256 devices in a mesh: space: 16 (over x_hi, z), tm: 16 (over x_lo, y, core).
Axes of the slice: x: 4 (x_hi: 2, x_lo: 2; x = x_hi * 2 + x_lo), y: 4, z: 8, core: 2. Of those that a mesh axis runs over, the one named last changes fastest.
Arguments:
- right_side: bfloat16 [16, 16, 4, 4, 64, 64], P('tm', 'space'), may hold values from -6 to 6
- batch_order: int32 [32], replicated, may hold values from 0 to 31, each once
- light_diag: bfloat16 [16, 16, 4, 4, 64, 128], P('tm', 'space'), may hold values from -1 to 2
- light_hops: bfloat16 [8, 16, 16, 4, 4, 64, 128], P(None, 'tm', 'space'), may hold values from -0.125 to 0.125
- charm_diag: bfloat16 [16, 16, 4, 4, 64, 128], P('tm', 'space'), may hold values from -1 to 2
- charm_hops: bfloat16 [8, 16, 16, 4, 4, 64, 128], P(None, 'tm', 'space'), may hold values from -0.125 to 0.125
- current_blocks: bfloat16 [16, 16, 4, 4, 64, 128], P('tm', 'space'), may hold values from -0.5 to 0.5
Outputs:
- light_field: bfloat16 [16, 16, 4, 4, 64, 64], P('tm', 'space')
- seq_field: bfloat16 [16, 16, 4, 4, 64, 64], P('tm', 'space')
- margin: float32 [2, 32, 32], replicated
The draws below stay inside these ranges and needn't reach their ends.
All inputs are finite; a program needn't handle non-finite values.
Results may differ from the reference program's by a relative error of at most 0.015.
Values may be sent and summed in bfloat16 or wider, within the bound.
A program may use at most 64 MiB of HBM per device.

```python
import math
import jax
import jax.numpy as jnp
from jax import lax

NC = 64
COLS = 32
LX = 4
LY = 4
SWEEPS = 4
NZ = 16
NT = 16


def block_draw(key, mass_term):
    block_shape = (NT, NZ, LX, LY, NC, NC)
    spread = 0.3 / math.sqrt(NC)
    key_real, key_imag = jax.random.split(key)
    real_part = jnp.clip(jax.random.normal(key_real, block_shape, jnp.float32), -5.0, 5.0) * spread
    imag_part = jnp.clip(jax.random.normal(key_imag, block_shape, jnp.float32), -5.0, 5.0) * spread
    identity = jnp.eye(NC, dtype=jnp.float32) * mass_term
    return jnp.concatenate([identity + real_part, imag_part], axis=-1).astype(jnp.bfloat16)


def draw_light_diag(key, part):
    return block_draw(jax.random.fold_in(key, 11), 1.0)


def draw_charm_diag(key, part):
    return block_draw(jax.random.fold_in(key, 23), 0.9)


def shard_levels(rng, extent, pieces, low, high):
    loudness, own = 1.0, jax.random.fold_in(rng, 6)
    for dim, blocks in pieces:
        draws = jnp.exp(jax.random.uniform(jax.random.fold_in(own, dim), (blocks,), jnp.float32, low / len(pieces), high / len(pieces)))
        loudness = loudness * jnp.repeat(draws, extent[dim] // blocks).reshape([-1 if axis == dim else 1 for axis in range(len(extent))])
    return loudness


def noise(own_key, dims, deviation, reach, pieces=(), held_as=jnp.bfloat16):
    entries = jax.random.normal(own_key, dims, jnp.float32) * deviation
    if len(pieces) > 0:
        entries = shard_levels(own_key, dims, pieces, -0.22, 0.18) * entries
    return jnp.clip(entries, min=-reach, max=reach).astype(held_as)


def setup_inputs(seed: int = 0) -> dict:
    arg_keys = jax.random.split(jax.random.key(seed), 8)
    return {
        "right_side": noise(arg_keys[0], (NT, NZ, LX, LY, NC, 2 * COLS), 1.0, 6.0, ((0, 16), (1, 16))),
        "batch_order": jax.random.permutation(arg_keys[1], COLS).astype(jnp.int32),
        "light_diag": draw_light_diag(jax.random.fold_in(arg_keys[7], 71), 0),
        "light_hops": noise(arg_keys[3], (8, NT, NZ, LX, LY, NC, 2 * NC), (36 * NC) ** -0.5, 0.125, ((1, 16), (2, 16))),
        "charm_diag": draw_charm_diag(jax.random.fold_in(arg_keys[7], 71), 0),
        "charm_hops": noise(arg_keys[5], (8, NT, NZ, LX, LY, NC, 2 * NC), (40 * NC) ** -0.5, 0.125, ((1, 16), (2, 16))),
        "current_blocks": noise(arg_keys[6], (NT, NZ, LX, LY, NC, 2 * NC), (2 * NC) ** -0.5, 0.5, ((0, 16), (1, 16))),
    }


def expand(spinor):
    columns = spinor.shape[-1] // 2
    real_part = spinor[..., :columns]
    imag_part = spinor[..., columns:]
    lower = jnp.concatenate([-imag_part, real_part], axis=-1)
    return jnp.concatenate([spinor, lower], axis=-2)

def apply_block(blocks, spinor):
    return jnp.einsum('tzxyij,tzxyjk->tzxyik', blocks.astype(jnp.float32), expand(spinor.astype(jnp.float32)))

def hop_terms(hop_blocks, spinor):
    moves = ((-1, 2), (1, 2), (-1, 3), (1, 3), (-1, 1), (1, 1), (-1, 0), (1, 0))
    accumulated = jnp.zeros(spinor.shape, jnp.float32)
    for number in range(8):
        roll_by, roll_axis = moves[number]
        shifted = jnp.roll(spinor, roll_by, axis=roll_axis)
        accumulated = accumulated + apply_block(hop_blocks[number], shifted)
    return accumulated

def solve_system(diag_inverse, hop_blocks, source):
    spinor = jnp.zeros(source.shape, jnp.bfloat16)
    for sweep_index in range(SWEEPS):
        residue = (source.astype(jnp.float32) + hop_terms(hop_blocks, spinor)).astype(jnp.bfloat16)
        spinor = apply_block(diag_inverse, residue).astype(jnp.bfloat16)
    return spinor

def reference(right_side, batch_order, light_diag, light_hops, charm_diag, charm_hops, current_blocks):
    column_index = jnp.concatenate([batch_order, batch_order + COLS]).astype(jnp.int32)
    source = jnp.take(right_side, column_index, axis=-1)
    light_field = solve_system(light_diag, light_hops, source)
    inserted = apply_block(current_blocks, light_field).astype(jnp.bfloat16)
    seq_field = solve_system(charm_diag, charm_hops, inserted)
    flat_light = light_field.reshape(-1, 2 * COLS)
    flat_seq = seq_field.reshape(-1, 2 * COLS)
    gram = lax.dot_general(flat_light, flat_seq, (((0,), (0,)), ((), ())), preferred_element_type=jnp.float32)
    real_sum = gram[:COLS, :COLS] + gram[COLS:, COLS:]
    imag_sum = gram[:COLS, COLS:] - gram[COLS:, :COLS]
    factor_norm = 1.0 / math.sqrt(NT * NZ * LX * LY * NC)
    margin = jnp.stack([real_sum, imag_sum]) * factor_norm
    return (light_field, seq_field, margin)
```

```python
import math

import jax
import jax.numpy as jnp
from jax import lax
from jax.experimental import pallas as pl
from jax.experimental.pallas import tpu as pltpu
from jax.sharding import PartitionSpec as P

BF = jnp.bfloat16
F32 = jnp.float32
MESH = pl.DeviceIdType.MESH

LX = 4
LY = 4
SITES = LX * LY
PAIRS = SITES // 2
NC = 64
COLS = 32
LANES = 4 * COLS
CHUNKS = 4
PER = PAIRS // CHUNKS
ROUNDS = 6

X_LO = 2
Y = 4
Z = 8
CORES = 2
X = 4
STAGES = ((CORES, 0), (Y, 2), (X, 6), (Z, 10))
SLOTS = 18


def sites_of(pair):
    x, h = divmod(pair, 2)
    return x * LY + h, x * LY + h + 2


def body_kernel(
    right_hbm, order_ref, ldiag_hbm, lhops_hbm, cdiag_hbm, chops_hbm, current_hbm,
    light_out, seq_out, margin_ref,
    right, ldiag, lhops, cdiag, chops, current,
    sent, halo, local, base, acc, light_t, light_v, seq_v, red,
    in_sem, out_sem, send_sem, recv_sem, red_send, red_recv,
):
    space = lax.axis_index("space")
    tm = lax.axis_index("tm")
    n_space = lax.axis_size("space")
    n_tm = lax.axis_size("tm")
    z = lax.rem(space, Z)
    core = lax.rem(tm, CORES)
    y = lax.rem(tm // CORES, Y)
    x = (space // Z) * X_LO + tm // (CORES * Y)

    def device(x_, y_, z_, core_):
        return ((x_ // X_LO) * Z + z_, (lax.rem(x_, X_LO) * Y + y_) * CORES + core_)

    def partner(stage, step):
        if stage == 0:
            return device(x, y, z, lax.rem(core + step, CORES))
        if stage == 1:
            return device(x, lax.rem(y + step, Y), z, core)
        if stage == 2:
            return device(lax.rem(x + step, X), y, z, core)
        return device(x, y, lax.rem(z + step, Z), core)

    takers = (
        (lax.rem(space + n_space - 1, n_space), tm),
        (lax.rem(space + 1, n_space), tm),
        (space, lax.rem(tm + n_tm - 1, n_tm)),
        (space, lax.rem(tm + 1, n_tm)),
    )

    loads = [
        pltpu.make_async_copy(src, dst, in_sem.at[i])
        for i, (src, dst) in enumerate((
            (right_hbm, right),
            (ldiag_hbm, ldiag),
            (lhops_hbm.at[pl.ds(0, 4)], lhops.at[pl.ds(0, 4)]),
            (lhops_hbm.at[pl.ds(4, 4)], lhops.at[pl.ds(4, 4)]),
            (current_hbm, current),
            (cdiag_hbm, cdiag),
            (chops_hbm.at[pl.ds(0, 4)], chops.at[pl.ds(0, 4)]),
            (chops_hbm.at[pl.ds(4, 4)], chops.at[pl.ds(4, 4)]),
        ))
    ]
    for copy in loads:
        copy.start()

    barrier = pltpu.get_barrier_semaphore()
    greeted = list(takers)
    for stage, (count, _) in enumerate(STAGES):
        greeted += [partner(stage, step) for step in range(1, count)]
    for other in greeted:
        pl.semaphore_signal(barrier, inc=1, device_id=other, device_id_type=MESH)

    lane = lax.broadcasted_iota(jnp.int32, (NC, LANES), 1)
    first = lax.rem(lane, 2 * COLS) < COLS
    low = lane < 2 * COLS

    def turn(v):
        rolled = pltpu.roll(v, 2 * COLS, axis=1)
        return jnp.where(low, -rolled, rolled)

    def swap(v):
        return jnp.where(first, pltpu.roll(v, 3 * COLS, axis=1), pltpu.roll(v, COLS, axis=1))

    def product(blocks, widened):
        out = jnp.dot(blocks, widened, preferred_element_type=F32)
        return jnp.where(first, out[:NC], out[NC:])

    def pair_blocks(ref, pair):
        one, two = sites_of(pair)
        return jnp.concatenate([ref[one], ref[two]], axis=0)

    def hop_blocks(ref, pair, numbers):
        return jnp.concatenate([pair_blocks(ref.at[e], pair) for e in numbers], axis=1)

    def on_site(ref, pair, field32):
        v32 = field32.astype(BF).astype(F32)
        widened = jnp.concatenate([v32.astype(BF), turn(v32).astype(BF)], axis=0)
        return product(pair_blocks(ref, pair), widened)

    def keep(round_, pair, field32):
        v32 = field32.astype(BF).astype(F32)
        v = v32.astype(BF)
        sent[round_, pair] = v
        swapped = swap(v32)
        local[pair, 0] = jnp.concatenate([v, turn(v32).astype(BF)], axis=0)
        local[pair, 1] = jnp.concatenate(
            [swapped.astype(BF), turn(swapped).astype(BF)], axis=0
        )

    def halo_copy(round_, direction, chunk):
        part = pl.ds(chunk * PER, PER)
        return pltpu.make_async_remote_copy(
            src_ref=sent.at[round_, part],
            dst_ref=halo.at[round_, direction, part],
            send_sem=send_sem.at[round_, direction, chunk],
            recv_sem=recv_sem.at[round_, direction, chunk],
            device_id=takers[direction],
            device_id_type=MESH,
        )

    def send(round_, chunk):
        for direction in range(4):
            halo_copy(round_, direction, chunk).start()

    def local_phase(hops):
        for pair in range(PAIRS):
            px, h = divmod(pair, 2)
            ahead = ((px + 1) % LX) * 2 + h
            behind = ((px - 1) % LX) * 2 + h
            beside = px * 2 + 1 - h
            widened = jnp.concatenate(
                [local[ahead, 0], local[behind, 0], local[beside, h], local[beside, 1 - h]], axis=0
            )
            acc[pair] = base[pair].astype(F32) + product(
                hop_blocks(hops, pair, (0, 1, 2, 3)), widened
            )

    def remote_pair(round_, hops, diag, pair):
        parts = []
        for direction in range(4):
            v = halo[round_, direction, pair]
            parts += [v, turn(v.astype(F32)).astype(BF)]
        residue = acc[pair] + product(
            hop_blocks(hops, pair, (4, 5, 6, 7)), jnp.concatenate(parts, axis=0)
        )
        return on_site(diag, pair, residue)

    def arrive(round_, chunk):
        for direction in range(4):
            halo_copy(round_, direction, chunk).wait_recv()

    def pairs_of(chunk):
        return range(chunk * PER, (chunk + 1) * PER)

    order = jnp.concatenate([order_ref[...]] * 4, axis=1)
    picked = order + jnp.where(low[:1], 0, COLS)
    row = lax.broadcasted_iota(jnp.int32, (2 * COLS, LANES), 0)
    hit = row == picked
    pick_one = jnp.where(jnp.logical_and(hit, first), 1.0, 0.0).astype(BF)
    pick_two = jnp.where(jnp.logical_and(hit, jnp.logical_not(first)), 1.0, 0.0).astype(BF)
    pick = jnp.concatenate([pick_one, pick_two], axis=0)

    loads[0].wait()
    loads[1].wait()
    for chunk in range(CHUNKS):
        for pair in pairs_of(chunk):
            one, two = sites_of(pair)
            both = jnp.dot(right[one], pick_one, preferred_element_type=F32) + jnp.dot(
                right[two], pick_two, preferred_element_type=F32
            )
            base[pair] = both.astype(BF)
            keep(0, pair, on_site(ldiag, pair, both))
        if chunk == 0:
            pl.semaphore_wait(barrier, SLOTS)
        send(0, chunk)
    loads[2].wait()
    loads[3].wait()

    def light_sweep(step, carry):
        local_phase(lhops)
        for chunk in range(CHUNKS):
            arrive(step, chunk)
            for pair in pairs_of(chunk):
                keep(step + 1, pair, remote_pair(step, lhops, ldiag, pair))
            send(step + 1, chunk)
        return carry

    lax.fori_loop(0, 2, light_sweep, 0)

    out_row = lax.broadcasted_iota(jnp.int32, (LANES, 2 * COLS), 0)
    out_col = lax.broadcasted_iota(jnp.int32, (LANES, 2 * COLS), 1)
    source_lane = lax.rem(out_col, COLS) + (out_col // COLS) * 2 * COLS
    take_one = jnp.where(out_row == source_lane, 1.0, 0.0).astype(BF)
    take_two = jnp.where(out_row == source_lane + COLS, 1.0, 0.0).astype(BF)

    def put(ref, pair, v):
        one, two = sites_of(pair)
        ref[one] = jnp.dot(v, take_one, preferred_element_type=F32).astype(BF)
        ref[two] = jnp.dot(v, take_two, preferred_element_type=F32).astype(BF)

    local_phase(lhops)
    for i in (4, 5):
        loads[i].wait()
    for chunk in range(CHUNKS):
        arrive(2, chunk)
        for pair in pairs_of(chunk):
            field = remote_pair(2, lhops, ldiag, pair)
            v = field.astype(BF)
            light_t[pair] = v
            inserted = on_site(current, pair, field)
            base[pair] = inserted.astype(BF)
            keep(3, pair, on_site(cdiag, pair, inserted))
        send(3, chunk)
    loads[6].wait()
    loads[7].wait()
    for pair in range(PAIRS):
        put(light_v, pair, light_t[pair])
    light_copy = pltpu.make_async_copy(light_v, light_out, out_sem.at[0])
    light_copy.start()

    def charm_sweep(step, carry):
        local_phase(chops)
        for chunk in range(CHUNKS):
            arrive(step, chunk)
            for pair in pairs_of(chunk):
                keep(step + 1, pair, remote_pair(step, chops, cdiag, pair))
            send(step + 1, chunk)
        return carry

    lax.fori_loop(3, 5, charm_sweep, 0)

    local_phase(chops)
    gram = jnp.zeros((LANES, LANES), F32)
    for chunk in range(CHUNKS):
        arrive(5, chunk)
        for pair in pairs_of(chunk):
            v = remote_pair(5, chops, cdiag, pair).astype(BF)
            gram = gram + lax.dot_general(
                light_t[pair], v, (((0,), (0,)), ((), ())), preferred_element_type=F32
            )
            put(seq_v, pair, v)
    seq_copy = pltpu.make_async_copy(seq_v, seq_out, out_sem.at[1])
    seq_copy.start()

    upper = gram[:COLS] + pltpu.roll(gram[COLS:2 * COLS], 3 * COLS, axis=1)
    lower = pltpu.roll(gram[2 * COLS:3 * COLS], 2 * COLS, axis=1) + pltpu.roll(
        gram[3 * COLS:], COLS, axis=1
    )
    sums = jnp.where(lane[:COLS] < COLS, upper + lower, upper - lower)
    half = COLS // 2
    total = jnp.where(
        first[:half], sums[:half], pltpu.roll(sums[half:], COLS, axis=1)
    )

    mine = (core, y, x, z)
    for stage, (count, offset) in enumerate(STAGES):
        me = mine[stage]
        red[offset + me] = total
        copies = []
        for step in range(1, count):
            copies.append(pltpu.make_async_remote_copy(
                src_ref=red.at[offset + me],
                dst_ref=red.at[offset + me],
                send_sem=red_send.at[offset + step],
                recv_sem=red_recv.at[offset + step],
                device_id=partner(stage, step),
                device_id_type=MESH,
            ))
        for copy in copies:
            copy.start()
        for copy in copies:
            copy.wait()
        total = red[offset]
        for slot in range(1, count):
            total = total + red[offset + slot]

    total = total * (1.0 / math.sqrt(n_space * n_tm * SITES * NC))
    margin_ref[0, :half] = total[:, :COLS]
    margin_ref[0, half:] = total[:, COLS:2 * COLS]
    margin_ref[1, :half] = total[:, 2 * COLS:3 * COLS]
    margin_ref[1, half:] = total[:, 3 * COLS:]

    light_copy.wait()
    seq_copy.wait()
    for round_ in range(ROUNDS):
        for chunk in range(CHUNKS):
            for direction in range(4):
                halo_copy(round_, direction, chunk).wait_send()


def body(right_side, batch_order, light_diag, light_hops, charm_diag, charm_hops, current_blocks):
    anywhere = pl.BlockSpec(memory_space=pl.ANY)
    vmem = pl.BlockSpec(memory_space=pltpu.VMEM)
    block = (SITES, NC, 2 * NC)
    field = (SITES, NC, 2 * COLS)
    hops = (8,) + block
    packed = (NC, LANES)
    light, seq, margin = pl.pallas_call(
        body_kernel,
        out_shape=(
            jax.ShapeDtypeStruct(field, BF),
            jax.ShapeDtypeStruct(field, BF),
            jax.ShapeDtypeStruct((2, COLS, COLS), F32),
        ),
        in_specs=[anywhere, vmem, anywhere, anywhere, anywhere, anywhere, anywhere],
        out_specs=(anywhere, anywhere, vmem),
        scratch_shapes=[
            pltpu.VMEM(field, BF),
            pltpu.VMEM(block, BF),
            pltpu.VMEM(hops, BF),
            pltpu.VMEM(block, BF),
            pltpu.VMEM(hops, BF),
            pltpu.VMEM(block, BF),
            pltpu.VMEM((ROUNDS, PAIRS) + packed, BF),
            pltpu.VMEM((ROUNDS, 4, PAIRS) + packed, BF),
            pltpu.VMEM((PAIRS, 2, 2 * NC, LANES), BF),
            pltpu.VMEM((PAIRS,) + packed, BF),
            pltpu.VMEM((PAIRS,) + packed, F32),
            pltpu.VMEM((PAIRS,) + packed, BF),
            pltpu.VMEM(field, BF),
            pltpu.VMEM(field, BF),
            pltpu.VMEM((SLOTS, COLS // 2, LANES), F32),
            pltpu.SemaphoreType.DMA((8,)),
            pltpu.SemaphoreType.DMA((2,)),
            pltpu.SemaphoreType.DMA((ROUNDS, 4, CHUNKS)),
            pltpu.SemaphoreType.DMA((ROUNDS, 4, CHUNKS)),
            pltpu.SemaphoreType.DMA((SLOTS,)),
            pltpu.SemaphoreType.DMA((SLOTS,)),
        ],
        compiler_params=pltpu.CompilerParams(
            collective_id=0, has_side_effects=True, vmem_limit_bytes=40 * 1024 * 1024
        ),
    )(
        right_side.reshape(field),
        batch_order.reshape(1, COLS),
        light_diag.reshape(block),
        light_hops.reshape(hops),
        charm_diag.reshape(block),
        charm_hops.reshape(hops),
        current_blocks.reshape(block),
    )
    shape = (1, 1, LX, LY, NC, 2 * COLS)
    return light.reshape(shape), seq.reshape(shape), margin


def solution(mesh):
    site = P("tm", "space", None, None, None, None)
    hop = P(None, "tm", "space", None, None, None, None)
    return jax.shard_map(
        body,
        mesh=mesh,
        in_specs=(site, P(), site, hop, site, hop, site),
        out_specs=(site, site, P()),
        check_vma=False,
    )
```

```python
import math

import jax
import jax.numpy as jnp
from jax import lax
from jax.experimental import pallas as pl
from jax.experimental.pallas import tpu as pltpu
from jax.sharding import PartitionSpec as P

BF = jnp.bfloat16
F32 = jnp.float32
MESH = pl.DeviceIdType.MESH

LX = 4
LY = 4
SITES = LX * LY
PAIRS = SITES // 2
NC = 64
COLS = 32
LANES = 4 * COLS
CHUNKS = 4
PER = PAIRS // CHUNKS
ROUNDS = 6

X_LO = 2
Y = 4
Z = 8
CORES = 2
X = 4
STAGES = ((CORES, 0), (Y, 2), (X, 6), (Z, 10))
SLOTS = 18


def sites_of(pair):
    x, h = divmod(pair, 2)
    return x * LY + h, x * LY + h + 2


def body_kernel(
    right_hbm, order_hbm, ldiag_hbm, lhops_hbm, cdiag_hbm, chops_hbm, current_hbm,
    light_out, seq_out, margin_ref,
    right, order_ref, ldiag, lhops, cdiag, chops, current,
    sent, halo, local, base, acc, light_t, red,
    in_sem, send_sem, recv_sem, red_send, red_recv,
):
    space = lax.axis_index("space")
    tm = lax.axis_index("tm")
    n_space = lax.axis_size("space")
    n_tm = lax.axis_size("tm")
    z = lax.rem(space, Z)
    core = lax.rem(tm, CORES)
    y = lax.rem(tm // CORES, Y)
    x = (space // Z) * X_LO + tm // (CORES * Y)

    def device(x_, y_, z_, core_):
        return ((x_ // X_LO) * Z + z_, (lax.rem(x_, X_LO) * Y + y_) * CORES + core_)

    def partner(stage, step):
        if stage == 0:
            return device(x, y, z, lax.rem(core + step, CORES))
        if stage == 1:
            return device(x, lax.rem(y + step, Y), z, core)
        if stage == 2:
            return device(lax.rem(x + step, X), y, z, core)
        return device(x, y, lax.rem(z + step, Z), core)

    takers = (
        (lax.rem(space + n_space - 1, n_space), tm),
        (lax.rem(space + 1, n_space), tm),
        (space, lax.rem(tm + n_tm - 1, n_tm)),
        (space, lax.rem(tm + 1, n_tm)),
    )

    loads = [
        pltpu.make_async_copy(src, dst, in_sem.at[i])
        for i, (src, dst) in enumerate((
            (right_hbm, right),
            (ldiag_hbm, ldiag),
            (lhops_hbm.at[pl.ds(0, 4)], lhops.at[pl.ds(0, 4)]),
            (lhops_hbm.at[pl.ds(4, 4)], lhops.at[pl.ds(4, 4)]),
            (current_hbm, current),
            (cdiag_hbm, cdiag),
            (chops_hbm.at[pl.ds(0, 4)], chops.at[pl.ds(0, 4)]),
            (chops_hbm.at[pl.ds(4, 4)], chops.at[pl.ds(4, 4)]),
            (order_hbm, order_ref),
        ))
    ]
    for copy in loads[-1:] + loads[:-1]:
        copy.start()

    barrier = pltpu.get_barrier_semaphore()
    greeted = list(takers)
    for stage, (count, _) in enumerate(STAGES):
        greeted += [partner(stage, step) for step in range(1, count)]
    for other in greeted:
        pl.semaphore_signal(barrier, inc=1, device_id=other, device_id_type=MESH)

    lane = lax.broadcasted_iota(jnp.int32, (NC, LANES), 1)
    first = lax.rem(lane, 2 * COLS) < COLS
    low = lane < 2 * COLS

    def turn(v):
        rolled = pltpu.roll(v, 2 * COLS, axis=1)
        return jnp.where(low, -rolled, rolled)

    def swap(v):
        return jnp.where(first, pltpu.roll(v, 3 * COLS, axis=1), pltpu.roll(v, COLS, axis=1))

    def product(blocks, widened):
        out = jnp.dot(blocks, widened, preferred_element_type=F32)
        return jnp.where(first, out[:NC], out[NC:])

    def pair_blocks(ref, pair):
        one, two = sites_of(pair)
        return jnp.concatenate([ref[one], ref[two]], axis=0)

    def hop_blocks(ref, pair, numbers):
        return jnp.concatenate([pair_blocks(ref.at[e], pair) for e in numbers], axis=1)

    def on_site(ref, pair, field32):
        v = field32.astype(BF)
        return product(pair_blocks(ref, pair), jnp.concatenate([v, turn(v)], axis=0))

    def keep(round_, pair, field32):
        v = field32.astype(BF)
        sent[round_, pair] = v
        swapped = swap(v)
        local[pair, 0] = jnp.concatenate([v, turn(v)], axis=0)
        local[pair, 1] = jnp.concatenate([swapped, turn(swapped)], axis=0)

    def halo_copy(round_, direction, chunk):
        part = pl.ds(chunk * PER, PER)
        return pltpu.make_async_remote_copy(
            src_ref=sent.at[round_, part],
            dst_ref=halo.at[round_, direction, part],
            send_sem=send_sem.at[round_, direction, chunk],
            recv_sem=recv_sem.at[round_, direction, chunk],
            device_id=takers[direction],
            device_id_type=MESH,
        )

    def send(round_, chunk):
        for direction in range(4):
            halo_copy(round_, direction, chunk).start()

    def local_phase(hops):
        for pair in range(PAIRS):
            px, h = divmod(pair, 2)
            ahead = ((px + 1) % LX) * 2 + h
            behind = ((px - 1) % LX) * 2 + h
            beside = px * 2 + 1 - h
            widened = jnp.concatenate(
                [local[ahead, 0], local[behind, 0], local[beside, h], local[beside, 1 - h]], axis=0
            )
            acc[pair] = base[pair].astype(F32) + product(
                hop_blocks(hops, pair, (0, 1, 2, 3)), widened
            )

    def remote_pair(round_, hops, diag, pair):
        parts = []
        for direction in range(4):
            v = halo[round_, direction, pair]
            parts += [v, turn(v)]
        residue = acc[pair] + product(
            hop_blocks(hops, pair, (4, 5, 6, 7)), jnp.concatenate(parts, axis=0)
        )
        return on_site(diag, pair, residue)

    def arrive(round_, chunk):
        for direction in range(4):
            halo_copy(round_, direction, chunk).wait_recv()

    def pairs_of(chunk):
        return range(chunk * PER, (chunk + 1) * PER)

    loads[8].wait()
    order = jnp.concatenate([order_ref[...]] * 4, axis=1)
    picked = order + jnp.where(low[:1], 0, COLS)
    row = lax.broadcasted_iota(jnp.int32, (2 * COLS, LANES), 0)
    hit = row == picked
    pick_one = jnp.where(jnp.logical_and(hit, first), 1.0, 0.0).astype(BF)
    pick_two = jnp.where(jnp.logical_and(hit, jnp.logical_not(first)), 1.0, 0.0).astype(BF)

    loads[0].wait()
    loads[1].wait()
    for chunk in range(CHUNKS):
        for pair in pairs_of(chunk):
            one, two = sites_of(pair)
            both = jnp.dot(right[one], pick_one, preferred_element_type=F32) + jnp.dot(
                right[two], pick_two, preferred_element_type=F32
            )
            base[pair] = both.astype(BF)
            keep(0, pair, on_site(ldiag, pair, both))
        if chunk == 0:
            pl.semaphore_wait(barrier, SLOTS)
        send(0, chunk)
    loads[2].wait()
    loads[3].wait()

    def light_sweep(step, carry):
        local_phase(lhops)
        for chunk in range(CHUNKS):
            arrive(step, chunk)
            for pair in pairs_of(chunk):
                keep(step + 1, pair, remote_pair(step, lhops, ldiag, pair))
            send(step + 1, chunk)
        return carry

    lax.fori_loop(0, 2, light_sweep, 0)

    out_row = lax.broadcasted_iota(jnp.int32, (LANES, 2 * COLS), 0)
    out_col = lax.broadcasted_iota(jnp.int32, (LANES, 2 * COLS), 1)
    source_lane = lax.rem(out_col, COLS) + (out_col // COLS) * 2 * COLS
    take_one = jnp.where(out_row == source_lane, 1.0, 0.0).astype(BF)
    take_two = jnp.where(out_row == source_lane + COLS, 1.0, 0.0).astype(BF)

    def put(ref, pair, v):
        one, two = sites_of(pair)
        ref[one] = jnp.dot(v, take_one, preferred_element_type=F32).astype(BF)
        ref[two] = jnp.dot(v, take_two, preferred_element_type=F32).astype(BF)

    local_phase(lhops)
    for i in (4, 5):
        loads[i].wait()
    for chunk in range(CHUNKS):
        arrive(2, chunk)
        for pair in pairs_of(chunk):
            field = remote_pair(2, lhops, ldiag, pair)
            v = field.astype(BF)
            light_t[pair] = v
            inserted = on_site(current, pair, field)
            base[pair] = inserted.astype(BF)
            keep(3, pair, on_site(cdiag, pair, inserted))
        send(3, chunk)
    loads[6].wait()
    loads[7].wait()
    for pair in range(PAIRS):
        put(light_out, pair, light_t[pair])

    def charm_sweep(step, carry):
        local_phase(chops)
        for chunk in range(CHUNKS):
            arrive(step, chunk)
            for pair in pairs_of(chunk):
                keep(step + 1, pair, remote_pair(step, chops, cdiag, pair))
            send(step + 1, chunk)
        return carry

    lax.fori_loop(3, 5, charm_sweep, 0)

    local_phase(chops)
    gram = jnp.zeros((LANES, LANES), F32)
    for chunk in range(CHUNKS):
        arrive(5, chunk)
        for pair in pairs_of(chunk):
            v = remote_pair(5, chops, cdiag, pair).astype(BF)
            gram = gram + lax.dot_general(
                light_t[pair], v, (((0,), (0,)), ((), ())), preferred_element_type=F32
            )
            put(seq_out, pair, v)

    upper = gram[:COLS] + pltpu.roll(gram[COLS:2 * COLS], 3 * COLS, axis=1)
    lower = pltpu.roll(gram[2 * COLS:3 * COLS], 2 * COLS, axis=1) + pltpu.roll(
        gram[3 * COLS:], COLS, axis=1
    )
    sums = jnp.where(lane[:COLS] < COLS, upper + lower, upper - lower)
    half = COLS // 2
    total = jnp.where(
        first[:half], sums[:half], pltpu.roll(sums[half:], COLS, axis=1)
    )

    mine = (core, y, x, z)
    for stage, (count, offset) in enumerate(STAGES):
        me = mine[stage]
        red[offset + me] = total
        copies = []
        for step in range(1, count):
            copies.append(pltpu.make_async_remote_copy(
                src_ref=red.at[offset + me],
                dst_ref=red.at[offset + me],
                send_sem=red_send.at[offset + step],
                recv_sem=red_recv.at[offset + step],
                device_id=partner(stage, step),
                device_id_type=MESH,
            ))
        for copy in copies:
            copy.start()
        for copy in copies:
            copy.wait()
        total = red[offset]
        for slot in range(1, count):
            total = total + red[offset + slot]

    total = total * (1.0 / math.sqrt(n_space * n_tm * SITES * NC))
    margin_ref[0, :half] = total[:, :COLS]
    margin_ref[0, half:] = total[:, COLS:2 * COLS]
    margin_ref[1, :half] = total[:, 2 * COLS:3 * COLS]
    margin_ref[1, half:] = total[:, 3 * COLS:]

    for round_ in range(ROUNDS):
        for chunk in range(CHUNKS):
            for direction in range(4):
                halo_copy(round_, direction, chunk).wait_send()


def finish_kernel(light_in, seq_in, margin_in, light_out, seq_out, margin_out, sem):
    copies = [
        pltpu.make_async_copy(src, dst, sem.at[i])
        for i, (src, dst) in enumerate(
            ((light_in, light_out), (seq_in, seq_out), (margin_in, margin_out))
        )
    ]
    for copy in copies:
        copy.start()
    for copy in copies:
        copy.wait()


def stay(array):
    return pltpu.with_memory_space_constraint(array, pltpu.HBM)


def body(right_side, batch_order, light_diag, light_hops, charm_diag, charm_hops, current_blocks):
    anywhere = pl.BlockSpec(memory_space=pl.ANY)
    vmem = pl.BlockSpec(memory_space=pltpu.VMEM)
    block = (SITES, NC, 2 * NC)
    field = (SITES, NC, 2 * COLS)
    hops = (8,) + block
    packed = (NC, LANES)
    light, seq, margin = pl.pallas_call(
        body_kernel,
        out_shape=(
            jax.ShapeDtypeStruct(field, BF),
            jax.ShapeDtypeStruct(field, BF),
            jax.ShapeDtypeStruct((2, COLS, COLS), F32),
        ),
        in_specs=[anywhere, anywhere, anywhere, anywhere, anywhere, anywhere, anywhere],
        out_specs=(vmem, vmem, vmem),
        scratch_shapes=[
            pltpu.VMEM(field, BF),
            pltpu.VMEM((1, COLS), jnp.int32),
            pltpu.VMEM(block, BF),
            pltpu.VMEM(hops, BF),
            pltpu.VMEM(block, BF),
            pltpu.VMEM(hops, BF),
            pltpu.VMEM(block, BF),
            pltpu.VMEM((ROUNDS, PAIRS) + packed, BF),
            pltpu.VMEM((ROUNDS, 4, PAIRS) + packed, BF),
            pltpu.VMEM((PAIRS, 2, 2 * NC, LANES), BF),
            pltpu.VMEM((PAIRS,) + packed, BF),
            pltpu.VMEM((PAIRS,) + packed, F32),
            pltpu.VMEM((PAIRS,) + packed, BF),
            pltpu.VMEM((SLOTS, COLS // 2, LANES), F32),
            pltpu.SemaphoreType.DMA((9,)),
            pltpu.SemaphoreType.DMA((ROUNDS, 4, CHUNKS)),
            pltpu.SemaphoreType.DMA((ROUNDS, 4, CHUNKS)),
            pltpu.SemaphoreType.DMA((SLOTS,)),
            pltpu.SemaphoreType.DMA((SLOTS,)),
        ],
        compiler_params=pltpu.CompilerParams(
            collective_id=0, has_side_effects=True, vmem_limit_bytes=32 * 1024 * 1024
        ),
    )(
        stay(right_side.reshape(field)),
        stay(batch_order.reshape(1, COLS)),
        stay(light_diag.reshape(block)),
        stay(light_hops.reshape(hops)),
        stay(charm_diag.reshape(block)),
        stay(charm_hops.reshape(hops)),
        stay(current_blocks.reshape(block)),
    )
    light, seq, margin = pl.pallas_call(
        finish_kernel,
        out_shape=(
            jax.ShapeDtypeStruct(field, BF),
            jax.ShapeDtypeStruct(field, BF),
            jax.ShapeDtypeStruct((2, COLS, COLS), F32),
        ),
        in_specs=[anywhere] * 3,
        out_specs=(anywhere,) * 3,
        scratch_shapes=[pltpu.SemaphoreType.DMA((3,))],
        compiler_params=pltpu.CompilerParams(vmem_limit_bytes=1024 * 1024),
    )(light, seq, margin)
    shape = (1, 1, LX, LY, NC, 2 * COLS)
    return light.reshape(shape), seq.reshape(shape), margin


def solution(mesh):
    site = P("tm", "space", None, None, None, None)
    hop = P(None, "tm", "space", None, None, None, None)
    return jax.shard_map(
        body,
        mesh=mesh,
        in_specs=(site, P(), site, hop, site, hop, site),
        out_specs=(site, site, P()),
        check_vma=False,
    )
```

```python
import math

import jax
import jax.numpy as jnp
from jax import lax
from jax.experimental import pallas as pl
from jax.experimental.pallas import tpu as pltpu
from jax.sharding import PartitionSpec as P

BF = jnp.bfloat16
F32 = jnp.float32
MESH = pl.DeviceIdType.MESH

LX = 4
LY = 4
SITES = LX * LY
PAIRS = SITES // 2
NC = 64
COLS = 32
LANES = 4 * COLS
CHUNKS = 4
PER = PAIRS // CHUNKS
ROUNDS = 6

X_LO = 2
Y = 4
Z = 8
CORES = 2
X = 4
STAGES = ((CORES, 0), (Y, 2), (X, 6), (Z, 10))
SLOTS = 18


def sites_of(pair):
    x, h = divmod(pair, 2)
    return x * LY + h, x * LY + h + 2


def body_kernel(
    right_hbm, order_hbm, ldiag_hbm, lhops_hbm, cdiag_hbm, chops_hbm, current_hbm,
    light_out, seq_out, margin_ref,
    right, order_ref, ldiag, lhops, cdiag, chops, current,
    sent, halo, local, base, acc, light_t, red,
    weight, gram_ref, pull, pull_sent, pull_halo, pull_send, pull_recv,
    in_sem, send_sem, recv_sem, red_send, red_recv,
):
    space = lax.axis_index("space")
    tm = lax.axis_index("tm")
    n_space = lax.axis_size("space")
    n_tm = lax.axis_size("tm")
    z = lax.rem(space, Z)
    core = lax.rem(tm, CORES)
    y = lax.rem(tm // CORES, Y)
    x = (space // Z) * X_LO + tm // (CORES * Y)

    def device(x_, y_, z_, core_):
        return ((x_ // X_LO) * Z + z_, (lax.rem(x_, X_LO) * Y + y_) * CORES + core_)

    def partner(stage, step):
        if stage == 0:
            return device(x, y, z, lax.rem(core + step, CORES))
        if stage == 1:
            return device(x, lax.rem(y + step, Y), z, core)
        if stage == 2:
            return device(lax.rem(x + step, X), y, z, core)
        return device(x, y, lax.rem(z + step, Z), core)

    takers = (
        (lax.rem(space + n_space - 1, n_space), tm),
        (lax.rem(space + 1, n_space), tm),
        (space, lax.rem(tm + n_tm - 1, n_tm)),
        (space, lax.rem(tm + 1, n_tm)),
    )

    loads = [
        pltpu.make_async_copy(src, dst, in_sem.at[i])
        for i, (src, dst) in enumerate((
            (right_hbm, right),
            (ldiag_hbm, ldiag),
            (lhops_hbm.at[pl.ds(0, 4)], lhops.at[pl.ds(0, 4)]),
            (lhops_hbm.at[pl.ds(4, 4)], lhops.at[pl.ds(4, 4)]),
            (current_hbm, current),
            (cdiag_hbm, cdiag),
            (chops_hbm.at[pl.ds(0, 4)], chops.at[pl.ds(0, 4)]),
            (chops_hbm.at[pl.ds(4, 4)], chops.at[pl.ds(4, 4)]),
            (order_hbm, order_ref),
        ))
    ]
    for copy in loads[-1:] + loads[:-1]:
        copy.start()

    barrier = pltpu.get_barrier_semaphore()
    greeted = list(takers)
    for stage, (count, _) in enumerate(STAGES):
        greeted += [partner(stage, step) for step in range(1, count)]
    for other in greeted:
        pl.semaphore_signal(barrier, inc=1, device_id=other, device_id_type=MESH)

    lane = lax.broadcasted_iota(jnp.int32, (NC, LANES), 1)
    first = lax.rem(lane, 2 * COLS) < COLS
    low = lane < 2 * COLS

    def turn(v):
        rolled = pltpu.roll(v, 2 * COLS, axis=1)
        return jnp.where(low, -rolled, rolled)

    def swap(v):
        return jnp.where(first, pltpu.roll(v, 3 * COLS, axis=1), pltpu.roll(v, COLS, axis=1))

    def product(blocks, widened):
        out = jnp.dot(blocks, widened, preferred_element_type=F32)
        return jnp.where(first, out[:NC], out[NC:])

    def pair_blocks(ref, pair):
        one, two = sites_of(pair)
        return jnp.concatenate([ref[one], ref[two]], axis=0)

    def hop_blocks(ref, pair, numbers):
        return jnp.concatenate([pair_blocks(ref.at[e], pair) for e in numbers], axis=1)

    def on_site(ref, pair, field32):
        v = field32.astype(BF)
        return product(pair_blocks(ref, pair), jnp.concatenate([v, turn(v)], axis=0))

    def keep(round_, pair, field32):
        v = field32.astype(BF)
        sent[round_, pair] = v
        swapped = swap(v)
        local[pair, 0] = jnp.concatenate([v, turn(v)], axis=0)
        local[pair, 1] = jnp.concatenate([swapped, turn(swapped)], axis=0)

    def halo_copy(round_, direction, chunk):
        part = pl.ds(chunk * PER, PER)
        return pltpu.make_async_remote_copy(
            src_ref=sent.at[round_, part],
            dst_ref=halo.at[round_, direction, part],
            send_sem=send_sem.at[round_, direction, chunk],
            recv_sem=recv_sem.at[round_, direction, chunk],
            device_id=takers[direction],
            device_id_type=MESH,
        )

    def send(round_, chunk):
        for direction in range(4):
            halo_copy(round_, direction, chunk).start()

    def local_phase(hops):
        for pair in range(PAIRS):
            px, h = divmod(pair, 2)
            ahead = ((px + 1) % LX) * 2 + h
            behind = ((px - 1) % LX) * 2 + h
            beside = px * 2 + 1 - h
            widened = jnp.concatenate(
                [local[ahead, 0], local[behind, 0], local[beside, h], local[beside, 1 - h]], axis=0
            )
            acc[pair] = base[pair].astype(F32) + product(
                hop_blocks(hops, pair, (0, 1, 2, 3)), widened
            )

    def remote_pair(round_, hops, diag, pair):
        parts = []
        for direction in range(4):
            v = halo[round_, direction, pair]
            parts += [v, turn(v)]
        residue = acc[pair] + product(
            hop_blocks(hops, pair, (4, 5, 6, 7)), jnp.concatenate(parts, axis=0)
        )
        return on_site(diag, pair, residue)

    def arrive(round_, chunk):
        for direction in range(4):
            halo_copy(round_, direction, chunk).wait_recv()

    def pairs_of(chunk):
        return range(chunk * PER, (chunk + 1) * PER)

    loads[8].wait()
    order = jnp.concatenate([order_ref[...]] * 4, axis=1)
    picked = order + jnp.where(low[:1], 0, COLS)
    row = lax.broadcasted_iota(jnp.int32, (2 * COLS, LANES), 0)
    hit = row == picked
    pick_one = jnp.where(jnp.logical_and(hit, first), 1.0, 0.0).astype(BF)
    pick_two = jnp.where(jnp.logical_and(hit, jnp.logical_not(first)), 1.0, 0.0).astype(BF)

    loads[0].wait()
    loads[1].wait()
    for chunk in range(CHUNKS):
        for pair in pairs_of(chunk):
            one, two = sites_of(pair)
            both = jnp.dot(right[one], pick_one, preferred_element_type=F32) + jnp.dot(
                right[two], pick_two, preferred_element_type=F32
            )
            base[pair] = both.astype(BF)
            keep(0, pair, on_site(ldiag, pair, both))
        if chunk == 0:
            pl.semaphore_wait(barrier, SLOTS)
        send(0, chunk)
    loads[2].wait()
    loads[3].wait()

    def light_sweep(step, carry):
        local_phase(lhops)
        for chunk in range(CHUNKS):
            arrive(step, chunk)
            for pair in pairs_of(chunk):
                keep(step + 1, pair, remote_pair(step, lhops, ldiag, pair))
            send(step + 1, chunk)
        return carry

    lax.fori_loop(0, 2, light_sweep, 0)

    out_row = lax.broadcasted_iota(jnp.int32, (LANES, 2 * COLS), 0)
    out_col = lax.broadcasted_iota(jnp.int32, (LANES, 2 * COLS), 1)
    source_lane = lax.rem(out_col, COLS) + (out_col // COLS) * 2 * COLS
    take_one = jnp.where(out_row == source_lane, 1.0, 0.0).astype(BF)
    take_two = jnp.where(out_row == source_lane + COLS, 1.0, 0.0).astype(BF)

    def put(ref, pair, v):
        one, two = sites_of(pair)
        ref[one] = jnp.dot(v, take_one, preferred_element_type=F32).astype(BF)
        ref[two] = jnp.dot(v, take_two, preferred_element_type=F32).astype(BF)

    local_phase(lhops)
    for i in (4, 5):
        loads[i].wait()
    for chunk in range(CHUNKS):
        arrive(2, chunk)
        for pair in pairs_of(chunk):
            field = remote_pair(2, lhops, ldiag, pair)
            v = field.astype(BF)
            light_t[pair] = v
            inserted = on_site(current, pair, field)
            base[pair] = inserted.astype(BF)
            keep(3, pair, on_site(cdiag, pair, inserted))
        send(3, chunk)
    loads[6].wait()
    loads[7].wait()
    for pair in range(PAIRS):
        put(light_out, pair, light_t[pair])

    def charm_sweep(step, carry):
        local_phase(chops)
        for chunk in range(CHUNKS):
            arrive(step, chunk)
            for pair in pairs_of(chunk):
                keep(step + 1, pair, remote_pair(step, chops, cdiag, pair))
            send(step + 1, chunk)
        return carry

    def site_rows(v, which):
        one = which * COLS
        return jnp.concatenate(
            [v[one:one + COLS], v[2 * COLS + one:3 * COLS + one]], axis=0
        )

    def adjoint(rows, blocks, high):
        out = jnp.dot(rows, blocks, preferred_element_type=F32)
        rolled = pltpu.roll(out, NC, axis=1)
        if high:
            return rolled[:COLS] + out[COLS:], rolled[COLS:] - out[:COLS]
        return out[:COLS] + rolled[COLS:], out[COLS:] - rolled[:COLS]

    def stack(one, two):
        return jnp.concatenate([one[0], two[0], one[1], two[1]], axis=0)

    low_tall = lax.broadcasted_iota(jnp.int32, (LANES, LANES), 1) < NC

    gram_ref[...] = jnp.zeros((LANES, LANES), F32)

    def weigh(px, carry):
        for h in range(2):
            across = jnp.transpose(light_t[px * 2 + h], (1, 0))
            halves = []
            for which in range(2):
                site = px * LY + h + 2 * which
                real, imag = adjoint(site_rows(across, which), cdiag[site], False)
                weight[site] = jnp.concatenate([real, imag], axis=0)[:, :NC].astype(BF)
                halves.append((real[:, :NC], imag[:, :NC]))
            gram_ref[...] += jnp.dot(
                stack(*halves).astype(BF), base[px * 2 + h], preferred_element_type=F32
            )
        return carry

    def plane(e, px, h_low, swap_low, swap_high):
        sides = []
        for high, h, swapped in ((False, h_low, swap_low), (True, 1 - h_low, swap_high)):
            both = [
                adjoint(weight[px * LY + h + 2 * i], chops[e, px * LY + h + 2 * i], high)
                for i in range(2)
            ]
            sides.append(stack(both[1], both[0]) if swapped else stack(both[0], both[1]))
        return jnp.where(low_tall, sides[0], sides[1])

    def weigh_remote(px, carry):
        for direction in range(4):
            pull_sent[direction, px] = plane(4 + direction, px, 0, False, False).astype(BF)
        return carry

    def pull_copy(direction):
        return pltpu.make_async_remote_copy(
            src_ref=pull_sent.at[direction],
            dst_ref=pull_halo.at[direction],
            send_sem=pull_send.at[direction],
            recv_sem=pull_recv.at[direction],
            device_id=takers[direction ^ 1],
            device_id_type=MESH,
        )

    def weigh_local(px, carry):
        pull[lax.rem(px + 1, LX)] += plane(0, px, 0, False, False)
        pull[lax.rem(px + LX - 1, LX)] += plane(1, px, 0, False, False)
        pull[px] += plane(2, px, 1, True, False) + plane(3, px, 1, False, True)
        return carry

    lax.fori_loop(0, LX, weigh, 0)
    lax.fori_loop(0, LX, weigh_remote, 0)
    for direction in range(4):
        pull_copy(direction).start()
    pull[...] = jnp.zeros((LX, LANES, LANES), F32)
    lax.fori_loop(0, LX, weigh_local, 0)

    lax.fori_loop(3, 5, charm_sweep, 0)

    for direction in range(4):
        pull_copy(direction).wait_recv()
    gram = gram_ref[...]
    for px in range(LX):
        pulled = pull[px]
        for direction in range(4):
            pulled = pulled + pull_halo[direction, px].astype(F32)
        field = jnp.concatenate([sent[5, px * 2], sent[5, px * 2 + 1]], axis=0)
        gram = gram + jnp.dot(pulled.astype(BF), field, preferred_element_type=F32)

    upper = gram[:COLS] + pltpu.roll(gram[COLS:2 * COLS], 3 * COLS, axis=1)
    lower = pltpu.roll(gram[2 * COLS:3 * COLS], 2 * COLS, axis=1) + pltpu.roll(
        gram[3 * COLS:], COLS, axis=1
    )
    sums = jnp.where(lane[:COLS] < COLS, upper + lower, upper - lower)
    half = COLS // 2
    total = jnp.where(
        first[:half], sums[:half], pltpu.roll(sums[half:], COLS, axis=1)
    )

    mine = (core, y, x, z)

    def reduce_copy(stage, step):
        slot = STAGES[stage][1] + mine[stage]
        return pltpu.make_async_remote_copy(
            src_ref=red.at[slot],
            dst_ref=red.at[slot],
            send_sem=red_send.at[STAGES[stage][1] + step],
            recv_sem=red_recv.at[STAGES[stage][1] + step],
            device_id=partner(stage, step),
            device_id_type=MESH,
        )

    def reduce_start(stage, total):
        count, offset = STAGES[stage]
        red[offset + mine[stage]] = total
        for step in range(1, count):
            reduce_copy(stage, step).start()

    def reduce_done(stage):
        count, offset = STAGES[stage]
        for step in range(1, count):
            reduce_copy(stage, step).wait_recv()
        total = red[offset]
        for slot in range(1, count):
            total = total + red[offset + slot]
        return total

    def last_chunk(chunk):
        arrive(5, chunk)
        for pair in pairs_of(chunk):
            put(seq_out, pair, remote_pair(5, chops, cdiag, pair).astype(BF))

    reduce_start(0, total)
    local_phase(chops)
    reduce_start(1, reduce_done(0))
    reduce_start(2, reduce_done(1))
    for chunk in range(CHUNKS):
        last_chunk(chunk)
    reduce_start(3, reduce_done(2))
    total = reduce_done(3)
    total = total * (1.0 / math.sqrt(n_space * n_tm * SITES * NC))
    margin_ref[0, :half] = total[:, :COLS]
    margin_ref[0, half:] = total[:, COLS:2 * COLS]
    margin_ref[1, :half] = total[:, 2 * COLS:3 * COLS]
    margin_ref[1, half:] = total[:, 3 * COLS:]

    for direction in range(4):
        pull_copy(direction).wait_send()
    for stage, (count, _) in enumerate(STAGES):
        for step in range(1, count):
            reduce_copy(stage, step).wait_send()
    for round_ in range(ROUNDS):
        for chunk in range(CHUNKS):
            for direction in range(4):
                halo_copy(round_, direction, chunk).wait_send()


def finish_kernel(light_in, seq_in, margin_in, light_out, seq_out, margin_out, sem):
    copies = [
        pltpu.make_async_copy(src, dst, sem.at[i])
        for i, (src, dst) in enumerate(
            ((light_in, light_out), (seq_in, seq_out), (margin_in, margin_out))
        )
    ]
    for copy in copies:
        copy.start()
    for copy in copies:
        copy.wait()


def stay(array):
    return pltpu.with_memory_space_constraint(array, pltpu.HBM)


def body(right_side, batch_order, light_diag, light_hops, charm_diag, charm_hops, current_blocks):
    anywhere = pl.BlockSpec(memory_space=pl.ANY)
    vmem = pl.BlockSpec(memory_space=pltpu.VMEM)
    block = (SITES, NC, 2 * NC)
    field = (SITES, NC, 2 * COLS)
    hops = (8,) + block
    packed = (NC, LANES)
    light, seq, margin = pl.pallas_call(
        body_kernel,
        out_shape=(
            jax.ShapeDtypeStruct(field, BF),
            jax.ShapeDtypeStruct(field, BF),
            jax.ShapeDtypeStruct((2, COLS, COLS), F32),
        ),
        in_specs=[anywhere, anywhere, anywhere, anywhere, anywhere, anywhere, anywhere],
        out_specs=(vmem, vmem, vmem),
        scratch_shapes=[
            pltpu.VMEM(field, BF),
            pltpu.VMEM((1, COLS), jnp.int32),
            pltpu.VMEM(block, BF),
            pltpu.VMEM(hops, BF),
            pltpu.VMEM(block, BF),
            pltpu.VMEM(hops, BF),
            pltpu.VMEM(block, BF),
            pltpu.VMEM((ROUNDS, PAIRS) + packed, BF),
            pltpu.VMEM((ROUNDS, 4, PAIRS) + packed, BF),
            pltpu.VMEM((PAIRS, 2, 2 * NC, LANES), BF),
            pltpu.VMEM((PAIRS,) + packed, BF),
            pltpu.VMEM((PAIRS,) + packed, F32),
            pltpu.VMEM((PAIRS,) + packed, BF),
            pltpu.VMEM((SLOTS, COLS // 2, LANES), F32),
            pltpu.VMEM((SITES, 2 * COLS, NC), BF),
            pltpu.VMEM((LANES, LANES), F32),
            pltpu.VMEM((LX, LANES, LANES), F32),
            pltpu.VMEM((4, LX, LANES, LANES), BF),
            pltpu.VMEM((4, LX, LANES, LANES), BF),
            pltpu.SemaphoreType.DMA((4,)),
            pltpu.SemaphoreType.DMA((4,)),
            pltpu.SemaphoreType.DMA((9,)),
            pltpu.SemaphoreType.DMA((ROUNDS, 4, CHUNKS)),
            pltpu.SemaphoreType.DMA((ROUNDS, 4, CHUNKS)),
            pltpu.SemaphoreType.DMA((SLOTS,)),
            pltpu.SemaphoreType.DMA((SLOTS,)),
        ],
        compiler_params=pltpu.CompilerParams(
            collective_id=0, has_side_effects=True, vmem_limit_bytes=32 * 1024 * 1024
        ),
    )(
        stay(right_side.reshape(field)),
        stay(batch_order.reshape(1, COLS)),
        stay(light_diag.reshape(block)),
        stay(light_hops.reshape(hops)),
        stay(charm_diag.reshape(block)),
        stay(charm_hops.reshape(hops)),
        stay(current_blocks.reshape(block)),
    )
    light, seq, margin = pl.pallas_call(
        finish_kernel,
        out_shape=(
            jax.ShapeDtypeStruct(field, BF),
            jax.ShapeDtypeStruct(field, BF),
            jax.ShapeDtypeStruct((2, COLS, COLS), F32),
        ),
        in_specs=[anywhere] * 3,
        out_specs=(anywhere,) * 3,
        scratch_shapes=[pltpu.SemaphoreType.DMA((3,))],
        compiler_params=pltpu.CompilerParams(vmem_limit_bytes=1024 * 1024),
    )(light, seq, margin)
    shape = (1, 1, LX, LY, NC, 2 * COLS)
    return light.reshape(shape), seq.reshape(shape), margin


def solution(mesh):
    site = P("tm", "space", None, None, None, None)
    hop = P(None, "tm", "space", None, None, None, None)
    return jax.shard_map(
        body,
        mesh=mesh,
        in_specs=(site, P(), site, hop, site, hop, site),
        out_specs=(site, site, P()),
        check_vma=False,
    )
```

```python
import math

import jax
import jax.numpy as jnp
from jax import lax
from jax.experimental import pallas as pl
from jax.experimental.pallas import tpu as pltpu
from jax.sharding import PartitionSpec as P

BF = jnp.bfloat16
F32 = jnp.float32
MESH = pl.DeviceIdType.MESH

LX = 4
LY = 4
SITES = LX * LY
PAIRS = SITES // 2
NC = 64
COLS = 32
LANES = 4 * COLS
CHUNKS = 4
PER = PAIRS // CHUNKS
ROUNDS = 6

X_LO = 2
Y = 4
Z = 8
CORES = 2
X = 4
STAGES = ((Y * CORES, 0), (X, 8), (Z, 12))
SLOTS = 20


def sites_of(pair):
    x, h = divmod(pair, 2)
    return x * LY + h, x * LY + h + 2


def body_kernel(
    right_hbm, order_hbm, ldiag_hbm, lhops_hbm, cdiag_hbm, chops_hbm, current_hbm,
    light_out, seq_out, margin_ref,
    right, order_ref, ldiag, lhops, cdiag, chops, current,
    sent, halo, local, base, acc, light_t, red,
    weight, gram_ref, pull, pull_sent, pull_halo, pull_send, pull_recv,
    in_sem, send_sem, recv_sem, red_send, red_recv,
):
    space = lax.axis_index("space")
    tm = lax.axis_index("tm")
    n_space = lax.axis_size("space")
    n_tm = lax.axis_size("tm")
    z = lax.rem(space, Z)
    core = lax.rem(tm, CORES)
    y = lax.rem(tm // CORES, Y)
    x = (space // Z) * X_LO + tm // (CORES * Y)

    def device(x_, y_, z_, core_):
        return ((x_ // X_LO) * Z + z_, (lax.rem(x_, X_LO) * Y + y_) * CORES + core_)

    def partner(stage, step):
        if stage == 0:
            row = lax.rem(y * CORES + core + step, Y * CORES)
            return device(x, row // CORES, z, lax.rem(row, CORES))
        if stage == 1:
            return device(lax.rem(x + step, X), y, z, core)
        return device(x, y, lax.rem(z + step, Z), core)

    takers = (
        (lax.rem(space + n_space - 1, n_space), tm),
        (lax.rem(space + 1, n_space), tm),
        (space, lax.rem(tm + n_tm - 1, n_tm)),
        (space, lax.rem(tm + 1, n_tm)),
    )

    loads = [
        pltpu.make_async_copy(src, dst, in_sem.at[i])
        for i, (src, dst) in enumerate((
            (right_hbm, right),
            (ldiag_hbm, ldiag),
            (lhops_hbm.at[pl.ds(0, 4)], lhops.at[pl.ds(0, 4)]),
            (lhops_hbm.at[pl.ds(4, 4)], lhops.at[pl.ds(4, 4)]),
            (current_hbm, current),
            (cdiag_hbm, cdiag),
            (chops_hbm.at[pl.ds(0, 4)], chops.at[pl.ds(0, 4)]),
            (chops_hbm.at[pl.ds(4, 4)], chops.at[pl.ds(4, 4)]),
            (order_hbm, order_ref),
        ))
    ]
    for copy in loads[-1:] + loads[:-1]:
        copy.start()

    barrier = pltpu.get_barrier_semaphore()
    greeted = list(takers)
    for stage, (count, _) in enumerate(STAGES):
        greeted += [partner(stage, step) for step in range(1, count)]
    for other in greeted:
        pl.semaphore_signal(barrier, inc=1, device_id=other, device_id_type=MESH)

    lane = lax.broadcasted_iota(jnp.int32, (NC, LANES), 1)
    first = lax.rem(lane, 2 * COLS) < COLS
    low = lane < 2 * COLS

    def turn(v):
        rolled = pltpu.roll(v, 2 * COLS, axis=1)
        return jnp.where(low, -rolled, rolled)

    def swap(v):
        return jnp.where(first, pltpu.roll(v, 3 * COLS, axis=1), pltpu.roll(v, COLS, axis=1))

    def product(blocks, widened):
        out = jnp.dot(blocks, widened, preferred_element_type=F32)
        return jnp.where(first, out[:NC], out[NC:])

    def pair_blocks(ref, pair):
        one, two = sites_of(pair)
        return jnp.concatenate([ref[one], ref[two]], axis=0)

    def hop_blocks(ref, pair, numbers):
        return jnp.concatenate([pair_blocks(ref.at[e], pair) for e in numbers], axis=1)

    def on_site(ref, pair, field32):
        v = field32.astype(BF)
        return product(pair_blocks(ref, pair), jnp.concatenate([v, turn(v)], axis=0))

    def keep(round_, pair, field32):
        v = field32.astype(BF)
        sent[round_, pair] = v
        swapped = swap(v)
        local[pair, 0] = jnp.concatenate([v, turn(v)], axis=0)
        local[pair, 1] = jnp.concatenate([swapped, turn(swapped)], axis=0)

    def halo_copy(round_, direction, chunk):
        part = pl.ds(chunk * PER, PER)
        return pltpu.make_async_remote_copy(
            src_ref=sent.at[round_, part],
            dst_ref=halo.at[round_, direction, part],
            send_sem=send_sem.at[round_, direction, chunk],
            recv_sem=recv_sem.at[round_, direction, chunk],
            device_id=takers[direction],
            device_id_type=MESH,
        )

    def send(round_, chunk):
        for direction in range(4):
            halo_copy(round_, direction, chunk).start()

    def local_phase(hops):
        for pair in range(PAIRS):
            px, h = divmod(pair, 2)
            ahead = ((px + 1) % LX) * 2 + h
            behind = ((px - 1) % LX) * 2 + h
            beside = px * 2 + 1 - h
            widened = jnp.concatenate(
                [local[ahead, 0], local[behind, 0], local[beside, h], local[beside, 1 - h]], axis=0
            )
            acc[pair] = base[pair].astype(F32) + product(
                hop_blocks(hops, pair, (0, 1, 2, 3)), widened
            )

    def remote_pair(round_, hops, diag, pair):
        parts = []
        for direction in range(4):
            v = halo[round_, direction, pair]
            parts += [v, turn(v)]
        residue = acc[pair] + product(
            hop_blocks(hops, pair, (4, 5, 6, 7)), jnp.concatenate(parts, axis=0)
        )
        return on_site(diag, pair, residue)

    def arrive(round_, chunk):
        for direction in range(4):
            halo_copy(round_, direction, chunk).wait_recv()

    def pairs_of(chunk):
        return range(chunk * PER, (chunk + 1) * PER)

    loads[8].wait()
    order = jnp.concatenate([order_ref[...]] * 4, axis=1)
    picked = order + jnp.where(low[:1], 0, COLS)
    row = lax.broadcasted_iota(jnp.int32, (2 * COLS, LANES), 0)
    hit = row == picked
    pick_one = jnp.where(jnp.logical_and(hit, first), 1.0, 0.0).astype(BF)
    pick_two = jnp.where(jnp.logical_and(hit, jnp.logical_not(first)), 1.0, 0.0).astype(BF)

    loads[0].wait()
    loads[1].wait()
    for chunk in range(CHUNKS):
        for pair in pairs_of(chunk):
            one, two = sites_of(pair)
            both = jnp.dot(right[one], pick_one, preferred_element_type=F32) + jnp.dot(
                right[two], pick_two, preferred_element_type=F32
            )
            base[pair] = both.astype(BF)
            keep(0, pair, on_site(ldiag, pair, both))
        if chunk == 0:
            pl.semaphore_wait(barrier, len(greeted))
        send(0, chunk)
    loads[2].wait()
    loads[3].wait()

    def light_sweep(step, carry):
        local_phase(lhops)
        for chunk in range(CHUNKS):
            arrive(step, chunk)
            for pair in pairs_of(chunk):
                keep(step + 1, pair, remote_pair(step, lhops, ldiag, pair))
            send(step + 1, chunk)
        return carry

    lax.fori_loop(0, 2, light_sweep, 0)

    out_row = lax.broadcasted_iota(jnp.int32, (LANES, 2 * COLS), 0)
    out_col = lax.broadcasted_iota(jnp.int32, (LANES, 2 * COLS), 1)
    source_lane = lax.rem(out_col, COLS) + (out_col // COLS) * 2 * COLS
    take_one = jnp.where(out_row == source_lane, 1.0, 0.0).astype(BF)
    take_two = jnp.where(out_row == source_lane + COLS, 1.0, 0.0).astype(BF)

    def put(ref, pair, v):
        one, two = sites_of(pair)
        ref[one] = jnp.dot(v, take_one, preferred_element_type=F32).astype(BF)
        ref[two] = jnp.dot(v, take_two, preferred_element_type=F32).astype(BF)

    local_phase(lhops)
    for i in (4, 5):
        loads[i].wait()
    for chunk in range(CHUNKS):
        arrive(2, chunk)
        for pair in pairs_of(chunk):
            field = remote_pair(2, lhops, ldiag, pair)
            v = field.astype(BF)
            light_t[pair] = v
            inserted = on_site(current, pair, field)
            base[pair] = inserted.astype(BF)
            keep(3, pair, on_site(cdiag, pair, inserted))
        send(3, chunk)
    loads[6].wait()
    loads[7].wait()
    for pair in range(PAIRS):
        put(light_out, pair, light_t[pair])

    def charm_sweep(step, carry):
        local_phase(chops)
        for chunk in range(CHUNKS):
            arrive(step, chunk)
            for pair in pairs_of(chunk):
                keep(step + 1, pair, remote_pair(step, chops, cdiag, pair))
            send(step + 1, chunk)
        return carry

    def site_rows(v, which):
        one = which * COLS
        return jnp.concatenate(
            [v[one:one + COLS], v[2 * COLS + one:3 * COLS + one]], axis=0
        )

    def adjoint(rows, blocks, high):
        out = jnp.dot(rows, blocks, preferred_element_type=F32)
        rolled = pltpu.roll(out, NC, axis=1)
        if high:
            return rolled[:COLS] + out[COLS:], rolled[COLS:] - out[:COLS]
        return out[:COLS] + rolled[COLS:], out[COLS:] - rolled[:COLS]

    def stack(one, two):
        return jnp.concatenate([one[0], two[0], one[1], two[1]], axis=0)

    low_tall = lax.broadcasted_iota(jnp.int32, (LANES, LANES), 1) < NC

    gram_ref[...] = jnp.zeros((LANES, LANES), F32)

    def weigh(px, carry):
        for h in range(2):
            across = jnp.transpose(light_t[px * 2 + h], (1, 0))
            halves = []
            for which in range(2):
                site = px * LY + h + 2 * which
                real, imag = adjoint(site_rows(across, which), cdiag[site], False)
                weight[site] = jnp.concatenate([real, imag], axis=0)[:, :NC].astype(BF)
                halves.append((real[:, :NC], imag[:, :NC]))
            gram_ref[...] += jnp.dot(
                stack(*halves).astype(BF), base[px * 2 + h], preferred_element_type=F32
            )
        return carry

    def plane(e, px, h_low, swap_low, swap_high):
        sides = []
        for high, h, swapped in ((False, h_low, swap_low), (True, 1 - h_low, swap_high)):
            both = [
                adjoint(weight[px * LY + h + 2 * i], chops[e, px * LY + h + 2 * i], high)
                for i in range(2)
            ]
            sides.append(stack(both[1], both[0]) if swapped else stack(both[0], both[1]))
        return jnp.where(low_tall, sides[0], sides[1])

    def weigh_remote(px, carry):
        for direction in range(4):
            pull_sent[direction, px] = plane(4 + direction, px, 0, False, False).astype(BF)
        return carry

    def pull_copy(direction):
        return pltpu.make_async_remote_copy(
            src_ref=pull_sent.at[direction],
            dst_ref=pull_halo.at[direction],
            send_sem=pull_send.at[direction],
            recv_sem=pull_recv.at[direction],
            device_id=takers[direction ^ 1],
            device_id_type=MESH,
        )

    def weigh_local(px, carry):
        pull[lax.rem(px + 1, LX)] += plane(0, px, 0, False, False)
        pull[lax.rem(px + LX - 1, LX)] += plane(1, px, 0, False, False)
        pull[px] += plane(2, px, 1, True, False) + plane(3, px, 1, False, True)
        return carry

    lax.fori_loop(0, LX, weigh, 0)
    lax.fori_loop(0, LX, weigh_remote, 0)
    for direction in range(4):
        pull_copy(direction).start()
    pull[...] = jnp.zeros((LX, LANES, LANES), F32)
    lax.fori_loop(0, LX, weigh_local, 0)

    lax.fori_loop(3, 5, charm_sweep, 0)

    for direction in range(4):
        pull_copy(direction).wait_recv()
    gram = gram_ref[...]
    for px in range(LX):
        pulled = pull[px]
        for direction in range(4):
            pulled = pulled + pull_halo[direction, px].astype(F32)
        field = jnp.concatenate([sent[5, px * 2], sent[5, px * 2 + 1]], axis=0)
        gram = gram + jnp.dot(pulled.astype(BF), field, preferred_element_type=F32)

    upper = gram[:COLS] + pltpu.roll(gram[COLS:2 * COLS], 3 * COLS, axis=1)
    lower = pltpu.roll(gram[2 * COLS:3 * COLS], 2 * COLS, axis=1) + pltpu.roll(
        gram[3 * COLS:], COLS, axis=1
    )
    sums = jnp.where(lane[:COLS] < COLS, upper + lower, upper - lower)
    half = COLS // 2
    total = jnp.where(
        first[:half], sums[:half], pltpu.roll(sums[half:], COLS, axis=1)
    )

    mine = (y * CORES + core, x, z)

    def reduce_copy(stage, step):
        slot = STAGES[stage][1] + mine[stage]
        return pltpu.make_async_remote_copy(
            src_ref=red.at[slot],
            dst_ref=red.at[slot],
            send_sem=red_send.at[STAGES[stage][1] + step],
            recv_sem=red_recv.at[STAGES[stage][1] + step],
            device_id=partner(stage, step),
            device_id_type=MESH,
        )

    def reduce_start(stage, total):
        count, offset = STAGES[stage]
        red[offset + mine[stage]] = total
        for step in range(1, count):
            reduce_copy(stage, step).start()

    def reduce_done(stage):
        count, offset = STAGES[stage]
        for step in range(1, count):
            reduce_copy(stage, step).wait_recv()
        total = red[offset]
        for slot in range(1, count):
            total = total + red[offset + slot]
        return total

    def last_chunk(chunk):
        arrive(5, chunk)
        for pair in pairs_of(chunk):
            put(seq_out, pair, remote_pair(5, chops, cdiag, pair).astype(BF))

    reduce_start(0, total)
    local_phase(chops)
    reduce_start(1, reduce_done(0))
    for chunk in range(2):
        last_chunk(chunk)
    reduce_start(2, reduce_done(1))
    for chunk in range(2, CHUNKS):
        last_chunk(chunk)
    total = reduce_done(2)
    total = total * (1.0 / math.sqrt(n_space * n_tm * SITES * NC))
    margin_ref[0, :half] = total[:, :COLS]
    margin_ref[0, half:] = total[:, COLS:2 * COLS]
    margin_ref[1, :half] = total[:, 2 * COLS:3 * COLS]
    margin_ref[1, half:] = total[:, 3 * COLS:]

    for direction in range(4):
        pull_copy(direction).wait_send()
    for stage, (count, _) in enumerate(STAGES):
        for step in range(1, count):
            reduce_copy(stage, step).wait_send()
    for round_ in range(ROUNDS):
        for chunk in range(CHUNKS):
            for direction in range(4):
                halo_copy(round_, direction, chunk).wait_send()


def finish_kernel(light_in, seq_in, margin_in, light_out, seq_out, margin_out, sem):
    copies = [
        pltpu.make_async_copy(src, dst, sem.at[i])
        for i, (src, dst) in enumerate(
            ((light_in, light_out), (seq_in, seq_out), (margin_in, margin_out))
        )
    ]
    for copy in copies:
        copy.start()
    for copy in copies:
        copy.wait()


def stay(array):
    return pltpu.with_memory_space_constraint(array, pltpu.HBM)


def body(right_side, batch_order, light_diag, light_hops, charm_diag, charm_hops, current_blocks):
    anywhere = pl.BlockSpec(memory_space=pl.ANY)
    vmem = pl.BlockSpec(memory_space=pltpu.VMEM)
    block = (SITES, NC, 2 * NC)
    field = (SITES, NC, 2 * COLS)
    hops = (8,) + block
    packed = (NC, LANES)
    light, seq, margin = pl.pallas_call(
        body_kernel,
        out_shape=(
            jax.ShapeDtypeStruct(field, BF),
            jax.ShapeDtypeStruct(field, BF),
            jax.ShapeDtypeStruct((2, COLS, COLS), F32),
        ),
        in_specs=[anywhere, anywhere, anywhere, anywhere, anywhere, anywhere, anywhere],
        out_specs=(vmem, vmem, vmem),
        scratch_shapes=[
            pltpu.VMEM(field, BF),
            pltpu.VMEM((1, COLS), jnp.int32),
            pltpu.VMEM(block, BF),
            pltpu.VMEM(hops, BF),
            pltpu.VMEM(block, BF),
            pltpu.VMEM(hops, BF),
            pltpu.VMEM(block, BF),
            pltpu.VMEM((ROUNDS, PAIRS) + packed, BF),
            pltpu.VMEM((ROUNDS, 4, PAIRS) + packed, BF),
            pltpu.VMEM((PAIRS, 2, 2 * NC, LANES), BF),
            pltpu.VMEM((PAIRS,) + packed, BF),
            pltpu.VMEM((PAIRS,) + packed, F32),
            pltpu.VMEM((PAIRS,) + packed, BF),
            pltpu.VMEM((SLOTS, COLS // 2, LANES), F32),
            pltpu.VMEM((SITES, 2 * COLS, NC), BF),
            pltpu.VMEM((LANES, LANES), F32),
            pltpu.VMEM((LX, LANES, LANES), F32),
            pltpu.VMEM((4, LX, LANES, LANES), BF),
            pltpu.VMEM((4, LX, LANES, LANES), BF),
            pltpu.SemaphoreType.DMA((4,)),
            pltpu.SemaphoreType.DMA((4,)),
            pltpu.SemaphoreType.DMA((9,)),
            pltpu.SemaphoreType.DMA((ROUNDS, 4, CHUNKS)),
            pltpu.SemaphoreType.DMA((ROUNDS, 4, CHUNKS)),
            pltpu.SemaphoreType.DMA((SLOTS,)),
            pltpu.SemaphoreType.DMA((SLOTS,)),
        ],
        compiler_params=pltpu.CompilerParams(
            collective_id=0, has_side_effects=True, vmem_limit_bytes=32 * 1024 * 1024
        ),
    )(
        stay(right_side.reshape(field)),
        stay(batch_order.reshape(1, COLS)),
        stay(light_diag.reshape(block)),
        stay(light_hops.reshape(hops)),
        stay(charm_diag.reshape(block)),
        stay(charm_hops.reshape(hops)),
        stay(current_blocks.reshape(block)),
    )
    light, seq, margin = pl.pallas_call(
        finish_kernel,
        out_shape=(
            jax.ShapeDtypeStruct(field, BF),
            jax.ShapeDtypeStruct(field, BF),
            jax.ShapeDtypeStruct((2, COLS, COLS), F32),
        ),
        in_specs=[anywhere] * 3,
        out_specs=(anywhere,) * 3,
        scratch_shapes=[pltpu.SemaphoreType.DMA((3,))],
        compiler_params=pltpu.CompilerParams(vmem_limit_bytes=1024 * 1024),
    )(light, seq, margin)
    shape = (1, 1, LX, LY, NC, 2 * COLS)
    return light.reshape(shape), seq.reshape(shape), margin


def solution(mesh):
    site = P("tm", "space", None, None, None, None)
    hop = P(None, "tm", "space", None, None, None, None)
    return jax.shard_map(
        body,
        mesh=mesh,
        in_specs=(site, P(), site, hop, site, hop, site),
        out_specs=(site, site, P()),
        check_vma=False,
    )
```

```python
import math

import jax
import jax.numpy as jnp
from jax import lax
from jax.experimental import pallas as pl
from jax.experimental.pallas import tpu as pltpu
from jax.sharding import PartitionSpec as P

BF = jnp.bfloat16
F32 = jnp.float32
MESH = pl.DeviceIdType.MESH

LX = 4
LY = 4
SITES = LX * LY
PAIRS = SITES // 2
NC = 64
COLS = 32
LANES = 4 * COLS
CHUNKS = 4
PER = PAIRS // CHUNKS
ROUNDS = 6

X_LO = 2
Y = 4
Z = 8
CORES = 2
X = 4
STAGES = ((Y * CORES, 0), (X, 8), (Z, 12))
SLOTS = 20


def sites_of(pair):
    x, h = divmod(pair, 2)
    return x * LY + h, x * LY + h + 2


def body_kernel(
    right_hbm, order_hbm, ldiag_hbm, lhops_hbm, cdiag_hbm, chops_hbm, current_hbm,
    light_out, seq_out, margin_ref,
    right, order_ref, ldiag, lhops, cdiag, chops, current,
    sent, halo, local, base, acc, light_t, red,
    weight, gram_ref, pull, pull_sent, pull_halo, pull_send, pull_recv,
    in_sem, send_sem, recv_sem, red_send, red_recv,
):
    space = lax.axis_index("space")
    tm = lax.axis_index("tm")
    n_space = lax.axis_size("space")
    n_tm = lax.axis_size("tm")
    z = lax.rem(space, Z)
    core = lax.rem(tm, CORES)
    y = lax.rem(tm // CORES, Y)
    x = (space // Z) * X_LO + tm // (CORES * Y)

    def device(x_, y_, z_, core_):
        return ((x_ // X_LO) * Z + z_, (lax.rem(x_, X_LO) * Y + y_) * CORES + core_)

    def partner(stage, step):
        if stage == 0:
            row = lax.rem(y * CORES + core + step, Y * CORES)
            return device(x, row // CORES, z, lax.rem(row, CORES))
        if stage == 1:
            return device(lax.rem(x + step, X), y, z, core)
        return device(x, y, lax.rem(z + step, Z), core)

    takers = (
        (lax.rem(space + n_space - 1, n_space), tm),
        (lax.rem(space + 1, n_space), tm),
        (space, lax.rem(tm + n_tm - 1, n_tm)),
        (space, lax.rem(tm + 1, n_tm)),
    )

    loads = [
        pltpu.make_async_copy(src, dst, in_sem.at[i])
        for i, (src, dst) in enumerate((
            (right_hbm, right),
            (ldiag_hbm, ldiag),
            (lhops_hbm.at[pl.ds(0, 4)], lhops.at[pl.ds(0, 4)]),
            (lhops_hbm.at[pl.ds(4, 4)], lhops.at[pl.ds(4, 4)]),
            (current_hbm, current),
            (cdiag_hbm, cdiag),
            (chops_hbm.at[pl.ds(0, 4)], chops.at[pl.ds(0, 4)]),
            (chops_hbm.at[pl.ds(4, 4)], chops.at[pl.ds(4, 4)]),
            (order_hbm, order_ref),
        ))
    ]
    for copy in loads[-1:] + loads[:-1]:
        copy.start()

    barrier = pltpu.get_barrier_semaphore()
    greeted = list(takers)
    for stage, (count, _) in enumerate(STAGES):
        greeted += [partner(stage, step) for step in range(1, count)]
    for other in greeted:
        pl.semaphore_signal(barrier, inc=1, device_id=other, device_id_type=MESH)

    lane = lax.broadcasted_iota(jnp.int32, (NC, LANES), 1)
    first = lax.rem(lane, 2 * COLS) < COLS
    low = lane < 2 * COLS

    def turn(v):
        rolled = pltpu.roll(v, 2 * COLS, axis=1)
        return jnp.where(low, -rolled, rolled)

    def swap(v):
        return jnp.where(first, pltpu.roll(v, 3 * COLS, axis=1), pltpu.roll(v, COLS, axis=1))

    def product(blocks, widened):
        out = jnp.dot(blocks, widened, preferred_element_type=F32)
        return jnp.where(first, out[:NC], out[NC:])

    def pair_blocks(ref, pair):
        one, two = sites_of(pair)
        return jnp.concatenate([ref[one], ref[two]], axis=0)

    def hop_blocks(ref, pair, numbers):
        return jnp.concatenate([pair_blocks(ref.at[e], pair) for e in numbers], axis=1)

    def on_site(ref, pair, field32):
        v = field32.astype(BF)
        return product(pair_blocks(ref, pair), jnp.concatenate([v, turn(v)], axis=0))

    def keep(round_, pair, field32):
        v = field32.astype(BF)
        sent[round_, pair] = v
        swapped = swap(v)
        local[pair, 0] = jnp.concatenate([v, turn(v)], axis=0)
        local[pair, 1] = jnp.concatenate([swapped, turn(swapped)], axis=0)

    def halo_copy(round_, direction, chunk):
        part = pl.ds(chunk * PER, PER)
        return pltpu.make_async_remote_copy(
            src_ref=sent.at[round_, part],
            dst_ref=halo.at[round_, direction, part],
            send_sem=send_sem.at[round_, direction, chunk],
            recv_sem=recv_sem.at[round_, direction, chunk],
            device_id=takers[direction],
            device_id_type=MESH,
        )

    def send(round_, chunk):
        for direction in range(4):
            halo_copy(round_, direction, chunk).start()

    def local_phase(hops):
        for pair in range(PAIRS):
            px, h = divmod(pair, 2)
            ahead = ((px + 1) % LX) * 2 + h
            behind = ((px - 1) % LX) * 2 + h
            beside = px * 2 + 1 - h
            widened = jnp.concatenate(
                [local[ahead, 0], local[behind, 0], local[beside, h], local[beside, 1 - h]], axis=0
            )
            acc[pair] = base[pair].astype(F32) + product(
                hop_blocks(hops, pair, (0, 1, 2, 3)), widened
            )

    def remote_pair(round_, hops, diag, pair):
        parts = []
        for direction in range(4):
            v = halo[round_, direction, pair]
            parts += [v, turn(v)]
        residue = acc[pair] + product(
            hop_blocks(hops, pair, (4, 5, 6, 7)), jnp.concatenate(parts, axis=0)
        )
        return on_site(diag, pair, residue)

    def arrive(round_, chunk):
        for direction in range(4):
            halo_copy(round_, direction, chunk).wait_recv()

    def pairs_of(chunk):
        return range(chunk * PER, (chunk + 1) * PER)

    loads[8].wait()
    order = jnp.concatenate([order_ref[...]] * 4, axis=1)
    picked = order + jnp.where(low[:1], 0, COLS)
    row = lax.broadcasted_iota(jnp.int32, (2 * COLS, LANES), 0)
    hit = row == picked
    pick_one = jnp.where(jnp.logical_and(hit, first), 1.0, 0.0).astype(BF)
    pick_two = jnp.where(jnp.logical_and(hit, jnp.logical_not(first)), 1.0, 0.0).astype(BF)

    loads[0].wait()
    loads[1].wait()
    for chunk in range(CHUNKS):
        for pair in pairs_of(chunk):
            one, two = sites_of(pair)
            both = jnp.dot(right[one], pick_one, preferred_element_type=F32) + jnp.dot(
                right[two], pick_two, preferred_element_type=F32
            )
            base[pair] = both.astype(BF)
            keep(0, pair, on_site(ldiag, pair, both))
        if chunk == 0:
            pl.semaphore_wait(barrier, len(greeted))
        send(0, chunk)
    loads[2].wait()
    loads[3].wait()

    def light_sweep(step, carry):
        local_phase(lhops)
        for chunk in range(CHUNKS):
            arrive(step, chunk)
            for pair in pairs_of(chunk):
                keep(step + 1, pair, remote_pair(step, lhops, ldiag, pair))
            send(step + 1, chunk)
        return carry

    lax.fori_loop(0, 2, light_sweep, 0)

    out_row = lax.broadcasted_iota(jnp.int32, (LANES, 2 * COLS), 0)
    out_col = lax.broadcasted_iota(jnp.int32, (LANES, 2 * COLS), 1)
    source_lane = lax.rem(out_col, COLS) + (out_col // COLS) * 2 * COLS
    take_one = jnp.where(out_row == source_lane, 1.0, 0.0).astype(BF)
    take_two = jnp.where(out_row == source_lane + COLS, 1.0, 0.0).astype(BF)

    def put(ref, pair, v):
        one, two = sites_of(pair)
        ref[one] = jnp.dot(v, take_one, preferred_element_type=F32).astype(BF)
        ref[two] = jnp.dot(v, take_two, preferred_element_type=F32).astype(BF)

    local_phase(lhops)
    for i in (4, 5):
        loads[i].wait()
    for chunk in range(CHUNKS):
        arrive(2, chunk)
        for pair in pairs_of(chunk):
            field = remote_pair(2, lhops, ldiag, pair)
            v = field.astype(BF)
            light_t[pair] = v
            inserted = on_site(current, pair, field)
            base[pair] = inserted.astype(BF)
            keep(3, pair, on_site(cdiag, pair, inserted))
        send(3, chunk)
    loads[6].wait()
    loads[7].wait()

    def charm_sweep(step, carry):
        local_phase(chops)
        for chunk in range(CHUNKS):
            arrive(step, chunk)
            for pair in pairs_of(chunk):
                keep(step + 1, pair, remote_pair(step, chops, cdiag, pair))
            send(step + 1, chunk)
        return carry

    def site_rows(v, which):
        one = which * COLS
        return jnp.concatenate(
            [v[one:one + COLS], v[2 * COLS + one:3 * COLS + one]], axis=0
        )

    def adjoint(rows, blocks, high):
        out = jnp.dot(rows, blocks, preferred_element_type=F32)
        rolled = pltpu.roll(out, NC, axis=1)
        if high:
            return rolled[:COLS] + out[COLS:], rolled[COLS:] - out[:COLS]
        return out[:COLS] + rolled[COLS:], out[COLS:] - rolled[:COLS]

    def stack(one, two):
        return jnp.concatenate([one[0], two[0], one[1], two[1]], axis=0)

    low_tall = lax.broadcasted_iota(jnp.int32, (LANES, LANES), 1) < NC

    gram_ref[...] = jnp.zeros((LANES, LANES), F32)

    def weigh(px, carry):
        for h in range(2):
            across = jnp.transpose(light_t[px * 2 + h], (1, 0))
            halves = []
            for which in range(2):
                site = px * LY + h + 2 * which
                real, imag = adjoint(site_rows(across, which), cdiag[site], False)
                weight[site] = jnp.concatenate([real, imag], axis=0)[:, :NC].astype(BF)
                halves.append((real[:, :NC], imag[:, :NC]))
            gram_ref[...] += jnp.dot(
                stack(*halves).astype(BF), base[px * 2 + h], preferred_element_type=F32
            )
        return carry

    def plane(e, px, h_low, swap_low, swap_high):
        sides = []
        for high, h, swapped in ((False, h_low, swap_low), (True, 1 - h_low, swap_high)):
            both = [
                adjoint(weight[px * LY + h + 2 * i], chops[e, px * LY + h + 2 * i], high)
                for i in range(2)
            ]
            sides.append(stack(both[1], both[0]) if swapped else stack(both[0], both[1]))
        return jnp.where(low_tall, sides[0], sides[1])

    def pull_copy(direction):
        return pltpu.make_async_remote_copy(
            src_ref=pull_sent.at[direction],
            dst_ref=pull_halo.at[direction],
            send_sem=pull_send.at[direction],
            recv_sem=pull_recv.at[direction],
            device_id=takers[direction ^ 1],
            device_id_type=MESH,
        )

    def weigh_local(px, carry):
        pull[lax.rem(px + 1, LX)] += plane(0, px, 0, False, False)
        pull[lax.rem(px + LX - 1, LX)] += plane(1, px, 0, False, False)
        pull[px] += plane(2, px, 1, True, False) + plane(3, px, 1, False, True)
        return carry

    for px in range(LX):
        weigh(px, 0)
    for direction in range(4):
        for px in range(LX):
            pull_sent[direction, px] = plane(4 + direction, px, 0, False, False).astype(BF)
        pull_copy(direction).start()
    pull[...] = jnp.zeros((LX, LANES, LANES), F32)
    lax.fori_loop(0, LX, weigh_local, 0)

    lax.fori_loop(3, 5, charm_sweep, 0)

    for direction in range(4):
        pull_copy(direction).wait_recv()
    gram = gram_ref[...]
    for px in range(LX):
        pulled = pull[px]
        for direction in range(4):
            pulled = pulled + pull_halo[direction, px].astype(F32)
        field = jnp.concatenate([sent[5, px * 2], sent[5, px * 2 + 1]], axis=0)
        gram = gram + jnp.dot(pulled.astype(BF), field, preferred_element_type=F32)

    upper = gram[:COLS] + pltpu.roll(gram[COLS:2 * COLS], 3 * COLS, axis=1)
    lower = pltpu.roll(gram[2 * COLS:3 * COLS], 2 * COLS, axis=1) + pltpu.roll(
        gram[3 * COLS:], COLS, axis=1
    )
    sums = jnp.where(lane[:COLS] < COLS, upper + lower, upper - lower)
    half = COLS // 2
    total = jnp.where(
        first[:half], sums[:half], pltpu.roll(sums[half:], COLS, axis=1)
    )

    mine = (y * CORES + core, x, z)

    def reduce_copy(stage, step):
        slot = STAGES[stage][1] + mine[stage]
        return pltpu.make_async_remote_copy(
            src_ref=red.at[slot],
            dst_ref=red.at[slot],
            send_sem=red_send.at[STAGES[stage][1] + step],
            recv_sem=red_recv.at[STAGES[stage][1] + step],
            device_id=partner(stage, step),
            device_id_type=MESH,
        )

    def reduce_start(stage, total):
        count, offset = STAGES[stage]
        red[offset + mine[stage]] = total
        for step in range(1, count):
            reduce_copy(stage, step).start()

    def reduce_done(stage):
        count, offset = STAGES[stage]
        for step in range(1, count):
            reduce_copy(stage, step).wait_recv()
        total = red[offset]
        for slot in range(1, count):
            total = total + red[offset + slot]
        return total

    def last_chunk(chunk):
        arrive(5, chunk)
        for pair in pairs_of(chunk):
            put(seq_out, pair, remote_pair(5, chops, cdiag, pair).astype(BF))

    reduce_start(0, total)
    local_phase(chops)
    reduce_start(1, reduce_done(0))
    for chunk in range(2):
        last_chunk(chunk)
    reduce_start(2, reduce_done(1))
    for chunk in range(2, CHUNKS):
        last_chunk(chunk)
    for pair in range(PAIRS):
        put(light_out, pair, light_t[pair])
    total = reduce_done(2)
    total = total * (1.0 / math.sqrt(n_space * n_tm * SITES * NC))
    margin_ref[0, :half] = total[:, :COLS]
    margin_ref[0, half:] = total[:, COLS:2 * COLS]
    margin_ref[1, :half] = total[:, 2 * COLS:3 * COLS]
    margin_ref[1, half:] = total[:, 3 * COLS:]

    for direction in range(4):
        pull_copy(direction).wait_send()
    for stage, (count, _) in enumerate(STAGES):
        for step in range(1, count):
            reduce_copy(stage, step).wait_send()
    for round_ in range(ROUNDS):
        for chunk in range(CHUNKS):
            for direction in range(4):
                halo_copy(round_, direction, chunk).wait_send()


def finish_kernel(light_in, seq_in, margin_in, light_out, seq_out, margin_out, sem):
    copies = [
        pltpu.make_async_copy(src, dst, sem.at[i])
        for i, (src, dst) in enumerate(
            ((light_in, light_out), (seq_in, seq_out), (margin_in, margin_out))
        )
    ]
    for copy in copies:
        copy.start()
    for copy in copies:
        copy.wait()


def stay(array):
    return pltpu.with_memory_space_constraint(array, pltpu.HBM)


def body(right_side, batch_order, light_diag, light_hops, charm_diag, charm_hops, current_blocks):
    anywhere = pl.BlockSpec(memory_space=pl.ANY)
    vmem = pl.BlockSpec(memory_space=pltpu.VMEM)
    block = (SITES, NC, 2 * NC)
    field = (SITES, NC, 2 * COLS)
    hops = (8,) + block
    packed = (NC, LANES)
    light, seq, margin = pl.pallas_call(
        body_kernel,
        out_shape=(
            jax.ShapeDtypeStruct(field, BF),
            jax.ShapeDtypeStruct(field, BF),
            jax.ShapeDtypeStruct((2, COLS, COLS), F32),
        ),
        in_specs=[anywhere, anywhere, anywhere, anywhere, anywhere, anywhere, anywhere],
        out_specs=(vmem, vmem, vmem),
        scratch_shapes=[
            pltpu.VMEM(field, BF),
            pltpu.VMEM((1, COLS), jnp.int32),
            pltpu.VMEM(block, BF),
            pltpu.VMEM(hops, BF),
            pltpu.VMEM(block, BF),
            pltpu.VMEM(hops, BF),
            pltpu.VMEM(block, BF),
            pltpu.VMEM((ROUNDS, PAIRS) + packed, BF),
            pltpu.VMEM((ROUNDS, 4, PAIRS) + packed, BF),
            pltpu.VMEM((PAIRS, 2, 2 * NC, LANES), BF),
            pltpu.VMEM((PAIRS,) + packed, BF),
            pltpu.VMEM((PAIRS,) + packed, F32),
            pltpu.VMEM((PAIRS,) + packed, BF),
            pltpu.VMEM((SLOTS, COLS // 2, LANES), F32),
            pltpu.VMEM((SITES, 2 * COLS, NC), BF),
            pltpu.VMEM((LANES, LANES), F32),
            pltpu.VMEM((LX, LANES, LANES), F32),
            pltpu.VMEM((4, LX, LANES, LANES), BF),
            pltpu.VMEM((4, LX, LANES, LANES), BF),
            pltpu.SemaphoreType.DMA((4,)),
            pltpu.SemaphoreType.DMA((4,)),
            pltpu.SemaphoreType.DMA((9,)),
            pltpu.SemaphoreType.DMA((ROUNDS, 4, CHUNKS)),
            pltpu.SemaphoreType.DMA((ROUNDS, 4, CHUNKS)),
            pltpu.SemaphoreType.DMA((SLOTS,)),
            pltpu.SemaphoreType.DMA((SLOTS,)),
        ],
        compiler_params=pltpu.CompilerParams(
            collective_id=0, has_side_effects=True, vmem_limit_bytes=32 * 1024 * 1024
        ),
    )(
        stay(right_side.reshape(field)),
        stay(batch_order.reshape(1, COLS)),
        stay(light_diag.reshape(block)),
        stay(light_hops.reshape(hops)),
        stay(charm_diag.reshape(block)),
        stay(charm_hops.reshape(hops)),
        stay(current_blocks.reshape(block)),
    )
    light, seq, margin = pl.pallas_call(
        finish_kernel,
        out_shape=(
            jax.ShapeDtypeStruct(field, BF),
            jax.ShapeDtypeStruct(field, BF),
            jax.ShapeDtypeStruct((2, COLS, COLS), F32),
        ),
        in_specs=[anywhere] * 3,
        out_specs=(anywhere,) * 3,
        scratch_shapes=[pltpu.SemaphoreType.DMA((3,))],
        compiler_params=pltpu.CompilerParams(vmem_limit_bytes=1024 * 1024),
    )(light, seq, margin)
    shape = (1, 1, LX, LY, NC, 2 * COLS)
    return light.reshape(shape), seq.reshape(shape), margin


def solution(mesh):
    site = P("tm", "space", None, None, None, None)
    hop = P(None, "tm", "space", None, None, None, None)
    return jax.shard_map(
        body,
        mesh=mesh,
        in_specs=(site, P(), site, hop, site, hop, site),
        out_specs=(site, site, P()),
        check_vma=False,
    )
```

```python
import math

import jax
import jax.numpy as jnp
from jax import lax
from jax.experimental import pallas as pl
from jax.experimental.pallas import tpu as pltpu
from jax.sharding import PartitionSpec as P

BF = jnp.bfloat16
F32 = jnp.float32
MESH = pl.DeviceIdType.MESH

LX = 4
LY = 4
SITES = LX * LY
PAIRS = SITES // 2
NC = 64
COLS = 32
LANES = 4 * COLS
CHUNKS = 4
PER = PAIRS // CHUNKS
ROUNDS = 6

X_LO = 2
Y = 4
Z = 8
CORES = 2
X = 4
STAGES = ((Y * CORES, 0), (X, 8), (Z, 12))
SLOTS = 20


def sites_of(pair):
    x, h = divmod(pair, 2)
    return x * LY + h, x * LY + h + 2


def body_kernel(
    right_hbm, order_hbm, ldiag_hbm, lhops_hbm, cdiag_hbm, chops_hbm, current_hbm,
    light_out, seq_out, margin_ref,
    right, order_ref, ldiag, lhops, cdiag, chops, current,
    sent, halo, local, base, acc, light_t, red,
    weight, gram_ref, pull, pull_sent, pull_halo, pull_send, pull_recv,
    in_sem, send_sem, recv_sem, red_send, red_recv,
):
    space = lax.axis_index("space")
    tm = lax.axis_index("tm")
    n_space = lax.axis_size("space")
    n_tm = lax.axis_size("tm")
    z = lax.rem(space, Z)
    core = lax.rem(tm, CORES)
    y = lax.rem(tm // CORES, Y)
    x = (space // Z) * X_LO + tm // (CORES * Y)

    def device(x_, y_, z_, core_):
        return ((x_ // X_LO) * Z + z_, (lax.rem(x_, X_LO) * Y + y_) * CORES + core_)

    def partner(stage, step):
        if stage == 0:
            row = lax.rem(y * CORES + core + step, Y * CORES)
            return device(x, row // CORES, z, lax.rem(row, CORES))
        if stage == 1:
            return device(lax.rem(x + step, X), y, z, core)
        return device(x, y, lax.rem(z + step, Z), core)

    takers = (
        (lax.rem(space + n_space - 1, n_space), tm),
        (lax.rem(space + 1, n_space), tm),
        (space, lax.rem(tm + n_tm - 1, n_tm)),
        (space, lax.rem(tm + 1, n_tm)),
    )

    loads = [
        pltpu.make_async_copy(src, dst, in_sem.at[i])
        for i, (src, dst) in enumerate((
            (right_hbm, right),
            (ldiag_hbm, ldiag),
            (lhops_hbm.at[pl.ds(0, 4)], lhops.at[pl.ds(0, 4)]),
            (lhops_hbm.at[pl.ds(4, 4)], lhops.at[pl.ds(4, 4)]),
            (current_hbm, current),
            (cdiag_hbm, cdiag),
            (chops_hbm.at[pl.ds(0, 4)], chops.at[pl.ds(0, 4)]),
            (chops_hbm.at[pl.ds(4, 4)], chops.at[pl.ds(4, 4)]),
            (order_hbm, order_ref),
        ))
    ]
    for copy in loads[-1:] + loads[:-1]:
        copy.start()

    barrier = pltpu.get_barrier_semaphore()
    greeted = list(takers)
    for stage, (count, _) in enumerate(STAGES):
        greeted += [partner(stage, step) for step in range(1, count)]
    for other in greeted:
        pl.semaphore_signal(barrier, inc=1, device_id=other, device_id_type=MESH)

    lane = lax.broadcasted_iota(jnp.int32, (NC, LANES), 1)
    first = lax.rem(lane, 2 * COLS) < COLS
    low = lane < 2 * COLS

    def turn(v):
        rolled = pltpu.roll(v, 2 * COLS, axis=1)
        return jnp.where(low, -rolled, rolled)

    def swap(v):
        return jnp.where(first, pltpu.roll(v, 3 * COLS, axis=1), pltpu.roll(v, COLS, axis=1))

    def product(blocks, widened):
        out = jnp.dot(blocks, widened, preferred_element_type=F32)
        return jnp.where(first, out[:NC], out[NC:])

    def pair_blocks(ref, pair):
        one, two = sites_of(pair)
        return jnp.concatenate([ref[one], ref[two]], axis=0)

    def hop_blocks(ref, pair, numbers):
        return jnp.concatenate([pair_blocks(ref.at[e], pair) for e in numbers], axis=1)

    def on_site(ref, pair, field32):
        v = field32.astype(BF)
        return product(pair_blocks(ref, pair), jnp.concatenate([v, turn(v)], axis=0))

    def keep(round_, pair, field32):
        v = field32.astype(BF)
        sent[round_, pair] = v
        swapped = swap(v)
        local[pair, 0] = jnp.concatenate([v, turn(v)], axis=0)
        local[pair, 1] = jnp.concatenate([swapped, turn(swapped)], axis=0)

    def halo_copy(round_, direction, chunk):
        part = pl.ds(chunk * PER, PER)
        return pltpu.make_async_remote_copy(
            src_ref=sent.at[round_, part],
            dst_ref=halo.at[round_, direction, part],
            send_sem=send_sem.at[round_, direction, chunk],
            recv_sem=recv_sem.at[round_, direction, chunk],
            device_id=takers[direction],
            device_id_type=MESH,
        )

    def send(round_, chunk):
        for direction in range(4):
            halo_copy(round_, direction, chunk).start()

    def local_phase(hops):
        for pair in range(PAIRS):
            px, h = divmod(pair, 2)
            ahead = ((px + 1) % LX) * 2 + h
            behind = ((px - 1) % LX) * 2 + h
            beside = px * 2 + 1 - h
            widened = jnp.concatenate(
                [local[ahead, 0], local[behind, 0], local[beside, h], local[beside, 1 - h]], axis=0
            )
            acc[pair] = base[pair].astype(F32) + product(
                hop_blocks(hops, pair, (0, 1, 2, 3)), widened
            )

    def remote_pair(round_, hops, diag, pair):
        parts = []
        for direction in range(4):
            v = halo[round_, direction, pair]
            parts += [v, turn(v)]
        residue = acc[pair] + product(
            hop_blocks(hops, pair, (4, 5, 6, 7)), jnp.concatenate(parts, axis=0)
        )
        return on_site(diag, pair, residue)

    def arrive(round_, chunk):
        for direction in range(4):
            halo_copy(round_, direction, chunk).wait_recv()

    def pairs_of(chunk):
        return range(chunk * PER, (chunk + 1) * PER)

    loads[8].wait()
    order = jnp.concatenate([order_ref[...]] * 4, axis=1)
    picked = order + jnp.where(low[:1], 0, COLS)
    row = lax.broadcasted_iota(jnp.int32, (2 * COLS, LANES), 0)
    hit = row == picked
    pick_one = jnp.where(jnp.logical_and(hit, first), 1.0, 0.0).astype(BF)
    pick_two = jnp.where(jnp.logical_and(hit, jnp.logical_not(first)), 1.0, 0.0).astype(BF)

    loads[0].wait()
    loads[1].wait()
    for chunk in range(CHUNKS):
        for pair in pairs_of(chunk):
            one, two = sites_of(pair)
            both = jnp.dot(right[one], pick_one, preferred_element_type=F32) + jnp.dot(
                right[two], pick_two, preferred_element_type=F32
            )
            base[pair] = both.astype(BF)
            keep(0, pair, on_site(ldiag, pair, both))
    pl.semaphore_wait(barrier, len(greeted))
    for chunk in range(CHUNKS):
        send(0, chunk)
    loads[2].wait()
    loads[3].wait()

    def light_sweep(step, carry):
        local_phase(lhops)
        for chunk in range(CHUNKS):
            arrive(step, chunk)
            for pair in pairs_of(chunk):
                keep(step + 1, pair, remote_pair(step, lhops, ldiag, pair))
            send(step + 1, chunk)
        return carry

    lax.fori_loop(0, 2, light_sweep, 0)

    out_row = lax.broadcasted_iota(jnp.int32, (LANES, 2 * COLS), 0)
    out_col = lax.broadcasted_iota(jnp.int32, (LANES, 2 * COLS), 1)
    source_lane = lax.rem(out_col, COLS) + (out_col // COLS) * 2 * COLS
    take_one = jnp.where(out_row == source_lane, 1.0, 0.0).astype(BF)
    take_two = jnp.where(out_row == source_lane + COLS, 1.0, 0.0).astype(BF)

    def put(ref, pair, v):
        one, two = sites_of(pair)
        ref[one] = jnp.dot(v, take_one, preferred_element_type=F32).astype(BF)
        ref[two] = jnp.dot(v, take_two, preferred_element_type=F32).astype(BF)

    local_phase(lhops)
    for i in (4, 5):
        loads[i].wait()
    for chunk in range(CHUNKS):
        arrive(2, chunk)
        for pair in pairs_of(chunk):
            field = remote_pair(2, lhops, ldiag, pair)
            v = field.astype(BF)
            light_t[pair] = v
            inserted = on_site(current, pair, field)
            base[pair] = inserted.astype(BF)
            keep(3, pair, on_site(cdiag, pair, inserted))
        send(3, chunk)
    loads[6].wait()
    loads[7].wait()

    def charm_sweep(step, carry):
        local_phase(chops)
        for chunk in range(CHUNKS):
            arrive(step, chunk)
            for pair in pairs_of(chunk):
                keep(step + 1, pair, remote_pair(step, chops, cdiag, pair))
            send(step + 1, chunk)
        return carry

    def site_rows(v, which):
        one = which * COLS
        return jnp.concatenate(
            [v[one:one + COLS], v[2 * COLS + one:3 * COLS + one]], axis=0
        )

    def adjoint(rows, blocks, high):
        out = jnp.dot(rows, blocks, preferred_element_type=F32)
        rolled = pltpu.roll(out, NC, axis=1)
        if high:
            return rolled[:COLS] + out[COLS:], rolled[COLS:] - out[:COLS]
        return out[:COLS] + rolled[COLS:], out[COLS:] - rolled[:COLS]

    def stack(one, two):
        return jnp.concatenate([one[0], two[0], one[1], two[1]], axis=0)

    low_tall = lax.broadcasted_iota(jnp.int32, (LANES, LANES), 1) < NC

    gram_ref[...] = jnp.zeros((LANES, LANES), F32)

    def weigh(px, carry):
        for h in range(2):
            across = jnp.transpose(light_t[px * 2 + h], (1, 0))
            halves = []
            for which in range(2):
                site = px * LY + h + 2 * which
                real, imag = adjoint(site_rows(across, which), cdiag[site], False)
                weight[site] = jnp.concatenate([real, imag], axis=0)[:, :NC].astype(BF)
                halves.append((real[:, :NC], imag[:, :NC]))
            gram_ref[...] += jnp.dot(
                stack(*halves).astype(BF), base[px * 2 + h], preferred_element_type=F32
            )
        return carry

    def plane(e, px, h_low, swap_low, swap_high):
        sides = []
        for high, h, swapped in ((False, h_low, swap_low), (True, 1 - h_low, swap_high)):
            both = [
                adjoint(weight[px * LY + h + 2 * i], chops[e, px * LY + h + 2 * i], high)
                for i in range(2)
            ]
            sides.append(stack(both[1], both[0]) if swapped else stack(both[0], both[1]))
        return jnp.where(low_tall, sides[0], sides[1])

    def pull_copy(direction):
        return pltpu.make_async_remote_copy(
            src_ref=pull_sent.at[direction],
            dst_ref=pull_halo.at[direction],
            send_sem=pull_send.at[direction],
            recv_sem=pull_recv.at[direction],
            device_id=takers[direction ^ 1],
            device_id_type=MESH,
        )

    def weigh_local(px, carry):
        pull[lax.rem(px + 1, LX)] += plane(0, px, 0, False, False)
        pull[lax.rem(px + LX - 1, LX)] += plane(1, px, 0, False, False)
        pull[px] += plane(2, px, 1, True, False) + plane(3, px, 1, False, True)
        return carry

    for px in range(LX):
        weigh(px, 0)
    for direction in range(4):
        for px in range(LX):
            pull_sent[direction, px] = plane(4 + direction, px, 0, False, False).astype(BF)
        pull_copy(direction).start()
    pull[...] = jnp.zeros((LX, LANES, LANES), F32)
    lax.fori_loop(0, LX, weigh_local, 0)

    lax.fori_loop(3, 5, charm_sweep, 0)

    for direction in range(4):
        pull_copy(direction).wait_recv()
    gram = gram_ref[...]
    for px in range(LX):
        pulled = pull[px]
        for direction in range(4):
            pulled = pulled + pull_halo[direction, px].astype(F32)
        field = jnp.concatenate([sent[5, px * 2], sent[5, px * 2 + 1]], axis=0)
        gram = gram + jnp.dot(pulled.astype(BF), field, preferred_element_type=F32)

    upper = gram[:COLS] + pltpu.roll(gram[COLS:2 * COLS], 3 * COLS, axis=1)
    lower = pltpu.roll(gram[2 * COLS:3 * COLS], 2 * COLS, axis=1) + pltpu.roll(
        gram[3 * COLS:], COLS, axis=1
    )
    sums = jnp.where(lane[:COLS] < COLS, upper + lower, upper - lower)
    half = COLS // 2
    total = jnp.where(
        first[:half], sums[:half], pltpu.roll(sums[half:], COLS, axis=1)
    )

    mine = (y * CORES + core, x, z)

    def reduce_copy(stage, step):
        slot = STAGES[stage][1] + mine[stage]
        return pltpu.make_async_remote_copy(
            src_ref=red.at[slot],
            dst_ref=red.at[slot],
            send_sem=red_send.at[STAGES[stage][1] + step],
            recv_sem=red_recv.at[STAGES[stage][1] + step],
            device_id=partner(stage, step),
            device_id_type=MESH,
        )

    def reduce_start(stage, total):
        count, offset = STAGES[stage]
        red[offset + mine[stage]] = total
        for step in range(1, count):
            reduce_copy(stage, step).start()

    def reduce_done(stage):
        count, offset = STAGES[stage]
        for step in range(1, count):
            reduce_copy(stage, step).wait_recv()
        total = red[offset]
        for slot in range(1, count):
            total = total + red[offset + slot]
        return total

    def last_chunk(chunk):
        arrive(5, chunk)
        for pair in pairs_of(chunk):
            put(seq_out, pair, remote_pair(5, chops, cdiag, pair).astype(BF))

    reduce_start(0, total)
    local_phase(chops)
    reduce_start(1, reduce_done(0))
    for chunk in range(2):
        last_chunk(chunk)
    reduce_start(2, reduce_done(1))
    for chunk in range(2, CHUNKS):
        last_chunk(chunk)
    for pair in range(PAIRS):
        put(light_out, pair, light_t[pair])
    total = reduce_done(2)
    total = total * (1.0 / math.sqrt(n_space * n_tm * SITES * NC))
    margin_ref[0, :half] = total[:, :COLS]
    margin_ref[0, half:] = total[:, COLS:2 * COLS]
    margin_ref[1, :half] = total[:, 2 * COLS:3 * COLS]
    margin_ref[1, half:] = total[:, 3 * COLS:]

    for direction in range(4):
        pull_copy(direction).wait_send()
    for stage, (count, _) in enumerate(STAGES):
        for step in range(1, count):
            reduce_copy(stage, step).wait_send()
    for round_ in range(ROUNDS):
        for chunk in range(CHUNKS):
            for direction in range(4):
                halo_copy(round_, direction, chunk).wait_send()


def finish_kernel(light_in, seq_in, margin_in, light_out, seq_out, margin_out, sem):
    copies = [
        pltpu.make_async_copy(src, dst, sem.at[i])
        for i, (src, dst) in enumerate(
            ((light_in, light_out), (seq_in, seq_out), (margin_in, margin_out))
        )
    ]
    for copy in copies:
        copy.start()
    for copy in copies:
        copy.wait()


def stay(array):
    return pltpu.with_memory_space_constraint(array, pltpu.HBM)


def body(right_side, batch_order, light_diag, light_hops, charm_diag, charm_hops, current_blocks):
    anywhere = pl.BlockSpec(memory_space=pl.ANY)
    vmem = pl.BlockSpec(memory_space=pltpu.VMEM)
    block = (SITES, NC, 2 * NC)
    field = (SITES, NC, 2 * COLS)
    hops = (8,) + block
    packed = (NC, LANES)
    light, seq, margin = pl.pallas_call(
        body_kernel,
        out_shape=(
            jax.ShapeDtypeStruct(field, BF),
            jax.ShapeDtypeStruct(field, BF),
            jax.ShapeDtypeStruct((2, COLS, COLS), F32),
        ),
        in_specs=[anywhere, anywhere, anywhere, anywhere, anywhere, anywhere, anywhere],
        out_specs=(vmem, vmem, vmem),
        scratch_shapes=[
            pltpu.VMEM(field, BF),
            pltpu.VMEM((1, COLS), jnp.int32),
            pltpu.VMEM(block, BF),
            pltpu.VMEM(hops, BF),
            pltpu.VMEM(block, BF),
            pltpu.VMEM(hops, BF),
            pltpu.VMEM(block, BF),
            pltpu.VMEM((ROUNDS, PAIRS) + packed, BF),
            pltpu.VMEM((ROUNDS, 4, PAIRS) + packed, BF),
            pltpu.VMEM((PAIRS, 2, 2 * NC, LANES), BF),
            pltpu.VMEM((PAIRS,) + packed, BF),
            pltpu.VMEM((PAIRS,) + packed, F32),
            pltpu.VMEM((PAIRS,) + packed, BF),
            pltpu.VMEM((SLOTS, COLS // 2, LANES), F32),
            pltpu.VMEM((SITES, 2 * COLS, NC), BF),
            pltpu.VMEM((LANES, LANES), F32),
            pltpu.VMEM((LX, LANES, LANES), F32),
            pltpu.VMEM((4, LX, LANES, LANES), BF),
            pltpu.VMEM((4, LX, LANES, LANES), BF),
            pltpu.SemaphoreType.DMA((4,)),
            pltpu.SemaphoreType.DMA((4,)),
            pltpu.SemaphoreType.DMA((9,)),
            pltpu.SemaphoreType.DMA((ROUNDS, 4, CHUNKS)),
            pltpu.SemaphoreType.DMA((ROUNDS, 4, CHUNKS)),
            pltpu.SemaphoreType.DMA((SLOTS,)),
            pltpu.SemaphoreType.DMA((SLOTS,)),
        ],
        compiler_params=pltpu.CompilerParams(
            collective_id=0, has_side_effects=True, vmem_limit_bytes=32 * 1024 * 1024
        ),
    )(
        stay(right_side.reshape(field)),
        stay(batch_order.reshape(1, COLS)),
        stay(light_diag.reshape(block)),
        stay(light_hops.reshape(hops)),
        stay(charm_diag.reshape(block)),
        stay(charm_hops.reshape(hops)),
        stay(current_blocks.reshape(block)),
    )
    light, seq, margin = pl.pallas_call(
        finish_kernel,
        out_shape=(
            jax.ShapeDtypeStruct(field, BF),
            jax.ShapeDtypeStruct(field, BF),
            jax.ShapeDtypeStruct((2, COLS, COLS), F32),
        ),
        in_specs=[anywhere] * 3,
        out_specs=(anywhere,) * 3,
        scratch_shapes=[pltpu.SemaphoreType.DMA((3,))],
        compiler_params=pltpu.CompilerParams(vmem_limit_bytes=1024 * 1024),
    )(light, seq, margin)
    shape = (1, 1, LX, LY, NC, 2 * COLS)
    return light.reshape(shape), seq.reshape(shape), margin


def solution(mesh):
    site = P("tm", "space", None, None, None, None)
    hop = P(None, "tm", "space", None, None, None, None)
    return jax.shard_map(
        body,
        mesh=mesh,
        in_specs=(site, P(), site, hop, site, hop, site),
        out_specs=(site, site, P()),
        check_vma=False,
    )
```
